32 devices in a mesh: row: 4 (over z), col: 8 (over y, x, core).
Axes of the slice: x: 2, y: 2, z: 4, core: 2. Of those that a mesh axis runs over, the one named last changes fastest.
Arguments:
- frames: float32 [512, 64, 1024], P(('row', 'col')), may hold values from -1 to 6
- class_index: int32 [64, 1024], P('row', 'col'), may hold values from 0 to 7
- surface_mask: int32 [64, 1024], P('row', 'col'), may hold values 0 or 1
- effusivity: float32 [8], replicated, may hold values from 0.5 to 2
- conductivity: float32 [8], replicated, may hold values from 0.2 to 1
Outputs:
- heat_flux: float32 [64, 1024, 512], P('row', 'col')
The draws below stay inside these ranges and needn't reach their ends.
All inputs are finite; a program needn't handle non-finite values. No bound on the sum of `surface_mask` on one device may be relied on, other than what follows from the above.
Results may differ from the reference program's by a relative error of at most 0.0003.
Values sent between devices are 32-bit elements; how exact they have to be, the bound alone decides.
A program may use at most 64 MiB of HBM per device.

```python
import math
import jax
import jax.numpy as jnp
from jax import lax

FRAMES = 512
NCLASS = 8
PASSES = 3
HEIGHT = 64
WIDTH = 1024


def draw_frames(key, part):
    amp_key = jax.random.fold_in(key, 11)
    onset_key = jax.random.fold_in(key, 23)
    noise_key = jax.random.fold_in(key, 37)
    amplitude = jnp.exp(jax.random.uniform(amp_key, (HEIGHT, WIDTH), jnp.float32, math.log(0.5), math.log(5.0)))
    onset = jax.random.randint(onset_key, (HEIGHT, WIDTH), 0, FRAMES // 2).astype(jnp.float32)
    times = jnp.arange(FRAMES, dtype=jnp.float32)[:, None, None]
    elapsed = jnp.maximum(times - onset[None], 0.0)
    started = jnp.where(times >= onset[None], 1.0, 0.0)
    ramp = jnp.sqrt(elapsed / (FRAMES - onset[None]))
    noise = 0.05 * jax.random.normal(noise_key, (FRAMES, HEIGHT, WIDTH), jnp.float32)
    jump_share = 0.3
    ramp_share = 0.6
    history = amplitude[None] * (ramp_share * ramp + jump_share * started + noise)
    return jnp.clip(history, -1.0, 6.0)


def plant(array, stream_key, low, top_value):
    index_at = [jax.random.randint(jax.random.fold_in(stream_key, axis), (), 0, length) for axis, length in enumerate(array.shape)]
    longest = array.shape.index(max(array.shape))
    neighbour = index_at[:longest] + [(index_at[longest] + 1) % array.shape[longest]] + index_at[longest + 1:]
    return array.at[tuple(index_at)].set(low).at[tuple(neighbour)].set(top_value)


def setup_inputs(seed: int = 0) -> dict:
    key_of = jax.random.split(jax.random.key(seed), 6)
    frames = draw_frames(jax.random.fold_in(key_of[5], 71), 0)
    class_index = plant(jax.random.randint(key_of[1], (HEIGHT, WIDTH), 0, NCLASS), jax.random.fold_in(key_of[1], 1), 0, NCLASS - 1).astype(jnp.int32)
    surface_mask = plant((jax.random.randint(key_of[2], (HEIGHT, WIDTH), 0, 4) < 3).astype(jnp.int32), jax.random.fold_in(key_of[2], 1), 0, 1)
    effusivity = jnp.clip(jnp.exp(jax.random.uniform(key_of[3], (NCLASS,), jnp.float32, math.log(0.5), math.log(2.0))), 0.5, 2.0)
    conductivity = jnp.clip(jnp.exp(jax.random.uniform(key_of[4], (NCLASS,), jnp.float32, math.log(0.2), math.log(1.0))), 0.2, 1.0)
    return dict(frames=frames, class_index=class_index, surface_mask=surface_mask, effusivity=effusivity, conductivity=conductivity)


flux_factor = 1.1283791670955126
lateral_rate = 0.24

def weights(lagged):
    clipped = jnp.maximum(lagged, 0.0)
    return jnp.where(lagged >= 0.0, 1.0 / (jnp.sqrt(clipped) + jnp.sqrt(clipped + 1.0)), 0.0)

def kernel_from(later, earlier):
    lagged = (later[:, None] - earlier[None, :]).astype(jnp.float32)
    return weights(lagged) - weights(lagged - 1.0)

def reference(frames, class_index, surface_mask, effusivity, conductivity):
    frame_ids = jnp.arange(FRAMES, dtype=jnp.int32)
    kernel = kernel_from(frame_ids, frame_ids)
    convolved = lax.dot_general(frames, kernel, (((0,), (1,)), ((), ())), precision=lax.Precision.HIGHEST)
    maskf = surface_mask.astype(jnp.float32)
    gain = flux_factor * effusivity[class_index] * maskf
    lateral = lateral_rate * conductivity[class_index] * maskf
    heat_flux = convolved * gain[:, :, None]
    for pass_index in range(PASSES):
        padded = jnp.pad(heat_flux, ((1, 1), (1, 1), (0, 0)))
        center = padded[1:-1, 1:-1]
        laplace = padded[2:, 1:-1] + padded[:-2, 1:-1] + padded[1:-1, 2:] + padded[1:-1, :-2] - 4.0 * center
        heat_flux = center + lateral[:, :, None] * laplace
    return heat_flux
```

```python
import functools
import jax
import jax.numpy as jnp
from jax import lax
from jax.experimental import pallas as pl
from jax.experimental.pallas import tpu as pltpu
from jax.sharding import PartitionSpec as P

PASSES = 3
PAD = 8
GROUP = 8
LANES = 128
MESH = pl.DeviceIdType.MESH

flux_factor = 1.1283791670955126
lateral_rate = 0.24


def extended(block, sides, width):
    for axis, dim in sides:
        count = lax.axis_size(axis)
        forward = [(i, i + 1) for i in range(count - 1)]
        backward = [(target, source) for source, target in forward]
        low = lax.ppermute(
            lax.slice_in_dim(block, block.shape[dim] - width, None, axis=dim), axis, forward
        )
        high = lax.ppermute(lax.slice_in_dim(block, 0, width, axis=dim), axis, backward)
        block = jnp.concatenate([low, block, high], axis=dim)
    return block


def weights(lagged):
    clipped = jnp.maximum(lagged, 0.0)
    return jnp.where(lagged >= 0.0, 1.0 / (jnp.sqrt(clipped) + jnp.sqrt(clipped + 1.0)), 0.0)


def kernel_from(later, earlier):
    lagged = (later[:, None] - earlier[None, :]).astype(jnp.float32)
    return weights(lagged) - weights(lagged - 1.0)


def relax_once(padded, lateral):
    center = padded[1:-1, 1:-1]
    laplace = (
        padded[2:, 1:-1] + padded[:-2, 1:-1] + padded[1:-1, 2:] + padded[1:-1, :-2] - 4.0 * center
    )
    return center + lateral[:, :, None] * laplace


def plain_device(frames, class_index, surface_mask, effusivity, conductivity):
    row_count = lax.axis_size("row")
    col_count = lax.axis_size("col")
    local_frames, height, width = frames.shape
    tile_rows = height // row_count
    tile_cols = width // col_count
    total_frames = local_frames * row_count * col_count
    frame_ids = jnp.arange(total_frames, dtype=jnp.int32)
    contract = (((0,), (1,)), ((), ()))
    kernel = kernel_from(frame_ids, frame_ids)
    blocks = frames.reshape(local_frames, row_count, tile_rows, col_count, tile_cols)
    blocks = blocks.transpose(0, 1, 3, 2, 4).reshape(
        local_frames, row_count * col_count, tile_rows, tile_cols
    )
    convolved = lax.dot_general(
        lax.all_to_all(blocks, ("row", "col"), split_axis=1, concat_axis=0, tiled=True)[:, 0],
        kernel,
        contract,
        precision=lax.Precision.HIGHEST,
    )
    classes = jnp.arange(effusivity.shape[0], dtype=jnp.int32)
    matches = (class_index[:, :, None] == classes[None, None, :]).astype(jnp.float32)
    maskf = surface_mask.astype(jnp.float32)
    gain = flux_factor * jnp.sum(matches * effusivity, axis=-1) * maskf
    lateral = lateral_rate * jnp.sum(matches * conductivity, axis=-1) * maskf
    heat_flux = convolved * gain[:, :, None]
    padded = extended(heat_flux, (("row", 0), ("col", 1)), PASSES)
    lateral_wide = extended(lateral, (("row", 0), ("col", 1)), PASSES - 1)
    for pass_index in range(PASSES):
        margin = PASSES - 1 - pass_index
        offset = PASSES - 1 - margin
        lateral_part = lateral_wide[
            offset : offset + tile_rows + 2 * margin, offset : offset + tile_cols + 2 * margin
        ]
        padded = relax_once(padded, lateral_part)
    return padded


SIDES = ((-1, 0), (1, 0), (0, -1), (0, 1), (-1, -1), (-1, 1), (1, -1), (1, 1))


def gather_kernel(
    rows, cols, tile_rows, tile_cols, local,
    frames, class_ref, mask_ref, eff_ref, cond_ref,
    flux, wide,
    held, lat, near, gain, mix_ref,
    send_sem, recv_sem, own_sem, lat_send, lat_recv, halo_send, halo_recv,
):
    row, col = lax.axis_index("row"), lax.axis_index("col")
    group = cols * local
    total = rows * group
    halo = PASSES

    def there(step, count, at):
        return (at + step >= 0) & (at + step < count)

    def exists(side):
        return there(side[0], rows, row) & there(side[1], cols, col)

    classes = class_ref[...]
    maskf = mask_ref[...].astype(jnp.float32)
    eff = jnp.zeros(classes.shape, jnp.float32)
    cond = jnp.zeros(classes.shape, jnp.float32)
    for k in range(eff_ref.shape[0]):
        eff = jnp.where(classes == k, eff_ref[k], eff)
        cond = jnp.where(classes == k, cond_ref[k], cond)
    gain_rows = flux_factor * eff * maskf
    lat_rows = lateral_rate * cond * maskf
    lat[...] = lat_rows
    near[...] = jnp.zeros_like(near)

    @pl.loop(0, tile_rows + 2 * halo)
    def _(h):
        flux[h] = jnp.zeros(flux.shape[1:], jnp.float32)

    barrier = pltpu.get_barrier_semaphore()
    for k in range(rows):
        @pl.loop(0 if k else 1, cols)
        def _(j, k=k):
            pl.semaphore_signal(
                barrier, inc=1,
                device_id=(lax.rem(row + k, rows), lax.rem(col + j, cols)),
                device_id_type=MESH,
            )
    pl.semaphore_wait(barrier, rows * cols - 1)

    def lat_copy(i):
        side = SIDES[i]
        return pltpu.make_async_remote_copy(
            src_ref=lat, dst_ref=near.at[i], send_sem=lat_send.at[i], recv_sem=lat_recv.at[i],
            device_id=(row + side[0], col + side[1]), device_id_type=MESH,
        )

    order = [rows // 2] + [k for k in range(rows) if k != rows // 2 and k] + [0]
    order = list(dict.fromkeys(order))
    for k in order:
        @pl.loop(0 if k else 1, cols)
        def _(j, k=k):
            to_row, to_col = lax.rem(row + k, rows), lax.rem(col + j, cols)
            pltpu.make_async_remote_copy(
                src_ref=frames.at[
                    :,
                    pl.ds(pl.multiple_of(to_row * tile_rows, tile_rows), tile_rows),
                    pl.ds(pl.multiple_of(to_col * tile_cols, tile_cols), tile_cols),
                ],
                dst_ref=held.at[pl.ds((row * cols + col) * local, local)],
                send_sem=send_sem, recv_sem=recv_sem.at[k],
                device_id=(to_row, to_col), device_id_type=MESH,
            ).start()
        if k == order[0]:
            for i, side in enumerate(SIDES):
                @pl.when(exists(side))
                def _(i=i):
                    lat_copy(i).start()
    own = pltpu.make_async_copy(
        frames.at[
            :,
            pl.ds(pl.multiple_of(row * tile_rows, tile_rows), tile_rows),
            pl.ds(pl.multiple_of(col * tile_cols, tile_cols), tile_cols),
        ],
        held.at[pl.ds((row * cols + col) * local, local)],
        own_sem,
    )
    own.start()

    for k in range(rows):
        shape = (group, total)
        earlier = lax.broadcasted_iota(jnp.int32, shape, 0) + k * group
        later = lax.broadcasted_iota(jnp.int32, shape, 1)
        lagged = (later - earlier).astype(jnp.float32)
        mix = weights(lagged) - weights(lagged - 1.0)
        high = mix.astype(jnp.bfloat16)
        mix_ref[0, k * group : (k + 1) * group] = high
        mix_ref[1, k * group : (k + 1) * group] = (mix - high.astype(jnp.float32)).astype(jnp.bfloat16)

    def upright(line):
        return jnp.transpose(jnp.broadcast_to(line, (tile_cols, tile_cols)))[:, :LANES]

    for h in range(tile_rows):
        gain[h] = upright(gain_rows[h : h + 1])
    for i, side in enumerate(SIDES):
        @pl.when(exists((-side[0], -side[1])))
        def _(i=i):
            lat_copy(i).wait_recv()
        @pl.when(exists(side))
        def _(i=i):
            lat_copy(i).wait_send()
    slot = {(-a, -b): i for i, (a, b) in enumerate(SIDES)}
    inside = slice(PAD, PAD + tile_cols)
    for h in range(-halo, tile_rows + halo):
        up = -1 if h < 0 else (1 if h >= tile_rows else 0)
        at = h - up * tile_rows
        def line(side):
            if side == (0, 0):
                return lat_rows[at : at + 1]
            return near[slot[side], at : at + 1, :]
        wide[h + halo, inside] = upright(line((up, 0)))
        wide[h + halo, 0:PAD] = upright(line((up, -1)))[tile_cols - PAD :]
        wide[h + halo, PAD + tile_cols :] = upright(line((up, 1)))[:PAD]

    def product(source, q):
        x = held[pl.ds(pl.multiple_of(source * group, group), group), q * GROUP : (q + 1) * GROUP, :]
        x = jnp.transpose(jnp.swapaxes(x, 0, 1), (0, 2, 1)).reshape(GROUP * tile_cols, group)
        high = x.astype(jnp.bfloat16)
        low = (x - high.astype(jnp.float32)).astype(jnp.bfloat16)
        at = pl.ds(pl.multiple_of(source * group, group), group)
        out = jnp.dot(high, mix_ref[0, at], preferred_element_type=jnp.float32)
        out += jnp.dot(low, mix_ref[0, at], preferred_element_type=jnp.float32)
        out += jnp.dot(high, mix_ref[1, at], preferred_element_type=jnp.float32)
        return out.reshape(GROUP, tile_cols, total)

    def part(q):
        return slice(halo + q * GROUP, halo + (q + 1) * GROUP)

    def arrived(k):
        if k == 0:
            own.wait()
            blocks = held.at[pl.ds(0, group - local)]
        else:
            blocks = held.at[pl.ds(0, group)]
        pltpu.make_async_copy(blocks, blocks, recv_sem.at[k]).wait()
        return lax.rem(row - k + rows, rows)

    visits = [k for k in order if k]
    visits = visits[:-1] + [0] + visits[-1:]
    for k in visits[:-1]:
        source = arrived(k)
        for q in range(tile_rows // GROUP):
            flux[part(q), inside] += product(source, q)

    col_spans = {-1: (PAD, PAD + tile_cols), 1: (tile_cols, 0)}

    def halo_copy(i):
        up, aside = SIDES[i]
        near_rows = halo if aside == 0 else halo - 1
        if up == 0:
            from_rows = to_rows = pl.ds(halo, tile_rows)
        elif up < 0:
            from_rows, to_rows = pl.ds(halo, near_rows), pl.ds(halo + tile_rows, near_rows)
        else:
            from_rows = pl.ds(halo + tile_rows - near_rows, near_rows)
            to_rows = pl.ds(halo - near_rows, near_rows)
        if aside == 0:
            from_cols = to_cols = pl.ds(PAD, tile_cols)
        else:
            from_cols = pl.ds(col_spans[aside][0], PAD)
            to_cols = pl.ds(col_spans[aside][1], PAD)
        return pltpu.make_async_remote_copy(
            src_ref=flux.at[from_rows, from_cols], dst_ref=flux.at[to_rows, to_cols],
            send_sem=halo_send.at[i], recv_sem=halo_recv.at[i],
            device_id=(row + up, col + aside), device_id_type=MESH,
        )

    def send_halo(i):
        @pl.when(exists(SIDES[i]))
        def _():
            halo_copy(i).start()

    source = arrived(visits[-1])
    last = tile_rows // GROUP - 1
    for q in range(last + 1):
        here = slice(q * GROUP, (q + 1) * GROUP)
        g = jnp.concatenate([gain[here]] * (total // LANES), axis=-1)
        flux[part(q), inside] = (flux[part(q), inside] + product(source, q)) * g
        for i, side in enumerate(SIDES):
            if (side[0] == -1 and q == 0) or (side[0] == 1 and q == last):
                send_halo(i)
    for i, side in enumerate(SIDES):
        if side[0] == 0:
            send_halo(i)

    sent = held.at[pl.ds(0, total - local)]
    pltpu.make_async_copy(sent, sent, send_sem).wait()
    for i, side in enumerate(SIDES):
        @pl.when(exists(side))
        def _(i=i):
            halo_copy(i).wait_send()
        @pl.when(exists((-side[0], -side[1])))
        def _(i=i):
            halo_copy(i).wait_recv()


def relax_kernel(flux, wide, out, first, second):
    source = flux
    count, width = flux.shape[0], flux.shape[1]
    for step, target in enumerate((first, second, out)):
        low, high = step + 1, count - step - 1
        edge = (1 + step, width - 1 - step) if target is not out else (PAD, width - PAD)
        for h in range(low, high):
            a, b = edge
            center = source[h, a:b, :]
            laplace = (
                source[h + 1, a:b, :] + source[h - 1, a:b, :]
                + source[h, a + 1 : b + 1, :] + source[h, a - 1 : b - 1, :] - 4.0 * center
            )
            value = center + wide[h, a:b, :] * laplace
            if target is out:
                out[h - PASSES] = value
            else:
                target[h, a:b, :] = value
        source = target


def per_device(frames, class_index, surface_mask, effusivity, conductivity):
    rows = lax.axis_size("row")
    cols = lax.axis_size("col")
    local, height, width = frames.shape
    tile_rows, tile_cols = height // rows, width // cols
    total = local * rows * cols
    if local % 8 or tile_rows % GROUP or tile_cols != LANES or total % LANES or (local * cols) % LANES:
        return plain_device(frames, class_index, surface_mask, effusivity, conductivity)
    high_rows, wide_cols = tile_rows + 2 * PASSES, tile_cols + 2 * PAD
    vmem = pl.BlockSpec(memory_space=pltpu.VMEM)
    smem = pl.BlockSpec(memory_space=pltpu.SMEM)
    dma = pltpu.SemaphoreType.DMA
    sides = len(SIDES)
    flux, wide = pl.pallas_call(
        functools.partial(gather_kernel, rows, cols, tile_rows, tile_cols, local),
        out_shape=(
            jax.ShapeDtypeStruct((high_rows, wide_cols, total), jnp.float32),
            jax.ShapeDtypeStruct((high_rows, wide_cols, LANES), jnp.float32),
        ),
        in_specs=[pl.BlockSpec(memory_space=pltpu.HBM), vmem, vmem, smem, smem],
        out_specs=(vmem, vmem),
        scratch_shapes=[
            pltpu.VMEM((total, tile_rows, tile_cols), jnp.float32),
            pltpu.VMEM((tile_rows, tile_cols), jnp.float32),
            pltpu.VMEM((sides, tile_rows, tile_cols), jnp.float32),
            pltpu.VMEM((tile_rows, tile_cols, LANES), jnp.float32),
            pltpu.VMEM((2, total, total), jnp.bfloat16),
            dma, dma((rows,)), dma, dma((sides,)), dma((sides,)), dma((sides,)), dma((sides,)),
        ],
        compiler_params=pltpu.CompilerParams(
            collective_id=0, has_side_effects=True, vmem_limit_bytes=40 * 2**20
        ),
        name="gather",
    )(frames, class_index, surface_mask, effusivity, conductivity)
    return pl.pallas_call(
        relax_kernel,
        out_shape=jax.ShapeDtypeStruct((tile_rows, tile_cols, total), jnp.float32),
        grid=(total // LANES,),
        in_specs=[
            pl.BlockSpec((high_rows, wide_cols, LANES), lambda n: (0, 0, n)),
            pl.BlockSpec((high_rows, wide_cols, LANES), lambda n: (0, 0, 0)),
        ],
        out_specs=pl.BlockSpec((tile_rows, tile_cols, LANES), lambda n: (0, 0, n)),
        scratch_shapes=[pltpu.VMEM((high_rows, wide_cols, LANES), jnp.float32)] * 2,
        compiler_params=pltpu.CompilerParams(vmem_limit_bytes=24 * 2**20),
        name="relax",
    )(flux, wide)


def solution(mesh):
    in_specs = (P(("row", "col"), None, None), P("row", "col"), P("row", "col"), P(), P())
    out_specs = P("row", "col", None)
    return jax.shard_map(
        per_device, mesh=mesh, in_specs=in_specs, out_specs=out_specs, check_vma=False
    )
```

```python
import functools
import jax
import jax.numpy as jnp
from jax import lax
from jax.experimental import pallas as pl
from jax.experimental.pallas import tpu as pltpu
from jax.sharding import PartitionSpec as P

PASSES = 3
PAD = 8
GROUP = 8
LANES = 128
MESH = pl.DeviceIdType.MESH

flux_factor = 1.1283791670955126
lateral_rate = 0.24


def extended(block, sides, width):
    for axis, dim in sides:
        count = lax.axis_size(axis)
        forward = [(i, i + 1) for i in range(count - 1)]
        backward = [(target, source) for source, target in forward]
        low = lax.ppermute(
            lax.slice_in_dim(block, block.shape[dim] - width, None, axis=dim), axis, forward
        )
        high = lax.ppermute(lax.slice_in_dim(block, 0, width, axis=dim), axis, backward)
        block = jnp.concatenate([low, block, high], axis=dim)
    return block


def weights(lagged):
    clipped = jnp.maximum(lagged, 0.0)
    return jnp.where(lagged >= 0.0, 1.0 / (jnp.sqrt(clipped) + jnp.sqrt(clipped + 1.0)), 0.0)


def kernel_from(later, earlier):
    lagged = (later[:, None] - earlier[None, :]).astype(jnp.float32)
    return weights(lagged) - weights(lagged - 1.0)


def relax_once(padded, lateral):
    center = padded[1:-1, 1:-1]
    laplace = (
        padded[2:, 1:-1] + padded[:-2, 1:-1] + padded[1:-1, 2:] + padded[1:-1, :-2] - 4.0 * center
    )
    return center + lateral[:, :, None] * laplace


def plain_device(frames, class_index, surface_mask, effusivity, conductivity):
    row_count = lax.axis_size("row")
    col_count = lax.axis_size("col")
    local_frames, height, width = frames.shape
    tile_rows = height // row_count
    tile_cols = width // col_count
    total_frames = local_frames * row_count * col_count
    frame_ids = jnp.arange(total_frames, dtype=jnp.int32)
    contract = (((0,), (1,)), ((), ()))
    kernel = kernel_from(frame_ids, frame_ids)
    blocks = frames.reshape(local_frames, row_count, tile_rows, col_count, tile_cols)
    blocks = blocks.transpose(0, 1, 3, 2, 4).reshape(
        local_frames, row_count * col_count, tile_rows, tile_cols
    )
    convolved = lax.dot_general(
        lax.all_to_all(blocks, ("row", "col"), split_axis=1, concat_axis=0, tiled=True)[:, 0],
        kernel,
        contract,
        precision=lax.Precision.HIGHEST,
    )
    classes = jnp.arange(effusivity.shape[0], dtype=jnp.int32)
    matches = (class_index[:, :, None] == classes[None, None, :]).astype(jnp.float32)
    maskf = surface_mask.astype(jnp.float32)
    gain = flux_factor * jnp.sum(matches * effusivity, axis=-1) * maskf
    lateral = lateral_rate * jnp.sum(matches * conductivity, axis=-1) * maskf
    heat_flux = convolved * gain[:, :, None]
    padded = extended(heat_flux, (("row", 0), ("col", 1)), PASSES)
    lateral_wide = extended(lateral, (("row", 0), ("col", 1)), PASSES - 1)
    for pass_index in range(PASSES):
        margin = PASSES - 1 - pass_index
        offset = PASSES - 1 - margin
        lateral_part = lateral_wide[
            offset : offset + tile_rows + 2 * margin, offset : offset + tile_cols + 2 * margin
        ]
        padded = relax_once(padded, lateral_part)
    return padded


SIDES = ((-1, 0), (1, 0), (0, -1), (0, 1), (-1, -1), (-1, 1), (1, -1), (1, 1))


def gather_kernel(
    rows, cols, tile_rows, tile_cols, local,
    frames, class_ref, mask_ref, eff_ref, cond_ref,
    flux, wide,
    held, lat, near, gain, mix_ref, edge, rim, strip, side_out, side_in,
    send_sem, recv_sem, own_sem, lat_send, lat_recv,
    strip_send, strip_recv, strip_own, relay_send, relay_recv, side_send, side_recv,
):
    row, col = lax.axis_index("row"), lax.axis_index("col")
    group = cols * local
    total = rows * group
    halo = PASSES
    mid = rows // 2
    half = row // mid

    def there(step, count, at):
        return (at + step >= 0) & (at + step < count)

    def exists(side):
        return there(side[0], rows, row) & there(side[1], cols, col)

    classes = class_ref[...]
    maskf = mask_ref[...].astype(jnp.float32)
    eff = jnp.zeros(classes.shape, jnp.float32)
    cond = jnp.zeros(classes.shape, jnp.float32)
    for k in range(eff_ref.shape[0]):
        eff = jnp.where(classes == k, eff_ref[k], eff)
        cond = jnp.where(classes == k, cond_ref[k], cond)
    gain_rows = flux_factor * eff * maskf
    lat_rows = lateral_rate * cond * maskf
    lat[0] = lat_rows
    lat[1] = gain_rows
    near[...] = jnp.zeros_like(near)

    @pl.loop(0, tile_rows + 2 * halo)
    def _(h):
        flux[h] = jnp.zeros(flux.shape[1:], jnp.float32)

    barrier = pltpu.get_barrier_semaphore()
    for k in range(rows):
        @pl.loop(0 if k else 1, cols)
        def _(j, k=k):
            pl.semaphore_signal(
                barrier, inc=1,
                device_id=(lax.rem(row + k, rows), lax.rem(col + j, cols)),
                device_id_type=MESH,
            )
    pl.semaphore_wait(barrier, rows * cols - 1)

    def lat_copy(i):
        side = SIDES[i]
        return pltpu.make_async_remote_copy(
            src_ref=lat, dst_ref=near.at[i], send_sem=lat_send.at[i], recv_sem=lat_recv.at[i],
            device_id=(row + side[0], col + side[1]), device_id_type=MESH,
        )

    def column(at):
        return pl.ds(pl.multiple_of(at * tile_cols, tile_cols), tile_cols)

    order = [rows // 2] + [k for k in range(rows) if k != rows // 2 and k] + [0]
    for k in order:
        @pl.loop(0 if k else 1, cols)
        def _(j, k=k):
            to_row, to_col = lax.rem(row + k, rows), lax.rem(col + j, cols)
            pltpu.make_async_remote_copy(
                src_ref=frames.at[
                    :, pl.ds(pl.multiple_of(to_row * tile_rows, tile_rows), tile_rows), column(to_col)
                ],
                dst_ref=held.at[pl.ds((row * cols + col) * local, local)],
                send_sem=send_sem, recv_sem=recv_sem.at[k],
                device_id=(to_row, to_col), device_id_type=MESH,
            ).start()
        if k == order[0]:
            for i, side in enumerate(SIDES):
                @pl.when(exists(side))
                def _(i=i):
                    lat_copy(i).start()
    own = pltpu.make_async_copy(
        frames.at[:, pl.ds(pl.multiple_of(row * tile_rows, tile_rows), tile_rows), column(col)],
        held.at[pl.ds((row * cols + col) * local, local)],
        own_sem,
    )
    own.start()

    strip_row = mid - 1 + half
    strip_from = pl.ds(pl.multiple_of(mid * tile_rows - GROUP * half, GROUP), GROUP)
    strip_at = strip.at[pl.ds(((row - half * mid) * cols + col) * local, local)]
    beside = row == strip_row

    def strip_copy(j):
        to_col = lax.rem(col + j, cols)
        return pltpu.make_async_remote_copy(
            src_ref=frames.at[:, strip_from, column(to_col)], dst_ref=strip_at,
            send_sem=strip_send, recv_sem=strip_recv.at[row - half * mid],
            device_id=(strip_row, to_col), device_id_type=MESH,
        )

    @pl.loop(1, cols)
    def _(j):
        strip_copy(j).start()

    strip_self = pltpu.make_async_copy(frames.at[:, strip_from, column(col)], strip_at, strip_own)

    @pl.when(beside)
    def _():
        strip_self.start()

    @pl.when(jnp.logical_not(beside))
    def _():
        strip_copy(0).start()

    for k in range(rows):
        shape = (group, total)
        earlier = lax.broadcasted_iota(jnp.int32, shape, 0) + k * group
        later = lax.broadcasted_iota(jnp.int32, shape, 1)
        lagged = (later - earlier).astype(jnp.float32)
        mix = weights(lagged) - weights(lagged - 1.0)
        high = mix.astype(jnp.bfloat16)
        mix_ref[0, k * group : (k + 1) * group] = high
        mix_ref[1, k * group : (k + 1) * group] = (mix - high.astype(jnp.float32)).astype(jnp.bfloat16)

    def upright(line):
        return jnp.transpose(jnp.broadcast_to(line, (tile_cols, tile_cols)))[:, :LANES]

    for i, side in enumerate(SIDES):
        @pl.when(exists((-side[0], -side[1])))
        def _(i=i):
            lat_copy(i).wait_recv()
        @pl.when(exists(side))
        def _(i=i):
            lat_copy(i).wait_send()
    slot = {(-a, -b): i for i, (a, b) in enumerate(SIDES)}
    inside = slice(PAD, PAD + tile_cols)
    for h in range(-halo, tile_rows + halo):
        up = -1 if h < 0 else (1 if h >= tile_rows else 0)
        at = h - up * tile_rows
        def line(side, which=0):
            if side == (0, 0):
                return lat[which, at : at + 1, :]
            return near[slot[side], which, at : at + 1, :]
        wide[h + halo, inside] = upright(line((up, 0)))
        wide[h + halo, 0:PAD] = upright(line((up, -1)))[tile_cols - PAD :]
        wide[h + halo, PAD + tile_cols :] = upright(line((up, 1)))[:PAD]
        gain[h + halo] = upright(line((up, 0), 1))

    def frames_of(source):
        return pl.ds(pl.multiple_of(source * group, group), group)

    def product(x, source):
        count = x.shape[0]
        x = jnp.transpose(x, (0, 2, 1)).reshape(count * tile_cols, group)
        high = x.astype(jnp.bfloat16)
        low = (x - high.astype(jnp.float32)).astype(jnp.bfloat16)
        at = frames_of(source)
        out = jnp.dot(high, mix_ref[0, at], preferred_element_type=jnp.float32)
        out += jnp.dot(low, mix_ref[0, at], preferred_element_type=jnp.float32)
        out += jnp.dot(high, mix_ref[1, at], preferred_element_type=jnp.float32)
        return out.reshape(count, tile_cols, total)

    def wait_for(ref, sem):
        pltpu.make_async_copy(ref, ref, sem).wait()

    def relayed(side, at_row, source):
        if side == 0:
            return (at_row >= 1) & jnp.logical_not((at_row == mid) & (source < mid))
        return (at_row < rows - 1) & jnp.logical_not((at_row == mid - 1) & (source >= mid))

    def relay_copy(side, k):
        source = lax.rem(row - k + rows, rows)
        at = frames_of(source)
        return pltpu.make_async_remote_copy(
            src_ref=edge.at[side, :, at], dst_ref=rim.at[1 - side, :, at],
            send_sem=relay_send.at[side, k], recv_sem=relay_recv.at[1 - side, k],
            device_id=(row + (1 if side else -1), col), device_id_type=MESH,
        )

    def full(value):
        return jnp.concatenate([value] * (total // LANES), axis=-1)

    last = tile_rows // GROUP - 1

    def main_part(k, finish):
        source = lax.rem(row - k + rows, rows)
        if k == 0:
            own.wait()
            wait_for(held.at[pl.ds(0, group - local)], recv_sem.at[k])
        else:
            wait_for(held.at[pl.ds(0, group)], recv_sem.at[k])
        at = frames_of(source)
        for q in range(last + 1):
            x = jnp.swapaxes(held[at, q * GROUP : (q + 1) * GROUP, :], 0, 1)
            if q == 0:
                edge[0, :, at] = x[:halo]
            if q == last:
                edge[1, :, at] = x[GROUP - halo :]
        for side in range(2):
            @pl.when(relayed(side, row, source))
            def _(side=side):
                relay_copy(side, k).start()
        for q in range(last + 1):
            x = jnp.swapaxes(held[at, q * GROUP : (q + 1) * GROUP, :], 0, 1)
            here = slice(halo + q * GROUP, halo + (q + 1) * GROUP)
            value = flux[here, inside] + product(x, source)
            flux[here, inside] = value * full(gain[here]) if finish else value

    def halo_part(k, finish):
        for side in range(2):
            beyond = row + (1 if side else -1)
            source = lax.rem(beyond - k + rows, rows)
            at = frames_of(source)
            here = slice(halo + tile_rows, 2 * halo + tile_rows) if side else slice(0, halo)

            @pl.when(there(1 if side else -1, rows, row))
            def _(side=side, beyond=beyond, source=source, at=at, here=here):
                direct = jnp.logical_not(relayed(1 - side, beyond, source))

                @pl.when(direct)
                def _():
                    turn = source - half * mid

                    @pl.when(source == row)
                    def _():
                        strip_self.wait()
                        wait_for(strip.at[pl.ds(0, group - local)], strip_recv.at[turn])

                    @pl.when(source != row)
                    def _():
                        wait_for(strip.at[pl.ds(0, group)], strip_recv.at[turn])

                    x = jnp.swapaxes(strip[frames_of(turn)], 0, 1)
                    rim[side, :, at] = x[:halo] if side else x[GROUP - halo :]

                @pl.when(jnp.logical_not(direct))
                def _():
                    wait_for(rim.at[side, :, at], relay_recv.at[side, k])

                value = flux[here, inside] + product(rim[side, :, at], source)
                flux[here, inside] = value * full(gain[here]) if finish else value

    visits = [k for k in order if k]
    visits = visits[:-1] + [0] + visits[-1:]
    for k in visits[:-1]:
        main_part(k, False)
    for k in visits[:-2]:
        halo_part(k, False)
    main_part(visits[-1], True)
    halo_part(visits[-2], False)
    halo_part(visits[-1], True)

    def side_copy(i):
        return pltpu.make_async_remote_copy(
            src_ref=side_out.at[i], dst_ref=side_in.at[1 - i],
            send_sem=side_send.at[i], recv_sem=side_recv.at[1 - i],
            device_id=(row, col + (1 if i else -1)), device_id_type=MESH,
        )

    for i in range(2):
        for j in range(halo):
            at = PAD + j + (tile_cols - halo if i else 0)
            side_out[i, j] = flux[:, at, :]
    for i in range(2):
        @pl.when(there(1 if i else -1, cols, col))
        def _(i=i):
            side_copy(i).start()

    wait_for(held.at[pl.ds(0, total - local)], send_sem)

    @pl.when(beside)
    def _():
        wait_for(strip.at[pl.ds(0, group - local)], strip_send)

    @pl.when(jnp.logical_not(beside))
    def _():
        wait_for(strip.at[pl.ds(0, group)], strip_send)

    for k in range(rows):
        for side in range(2):
            @pl.when(relayed(side, row, lax.rem(row - k + rows, rows)))
            def _(side=side, k=k):
                relay_copy(side, k).wait_send()
    for i in range(2):
        @pl.when(there(1 if i else -1, cols, col))
        def _(i=i):
            side_copy(i).wait_send()
            wait_for(side_in.at[i], side_recv.at[i])
            for j in range(halo):
                at = PAD + tile_cols + j if i else PAD - halo + j
                flux[:, at, :] = side_in[i, j]


def relax_kernel(flux, wide, out, first, second):
    source = flux
    count, width = flux.shape[0], flux.shape[1]
    for step, target in enumerate((first, second, out)):
        low, high = step + 1, count - step - 1
        edge = (1 + step, width - 1 - step) if target is not out else (PAD, width - PAD)
        for h in range(low, high):
            a, b = edge
            center = source[h, a:b, :]
            laplace = (
                source[h + 1, a:b, :] + source[h - 1, a:b, :]
                + source[h, a + 1 : b + 1, :] + source[h, a - 1 : b - 1, :] - 4.0 * center
            )
            value = center + wide[h, a:b, :] * laplace
            if target is out:
                out[h - PASSES] = value
            else:
                target[h, a:b, :] = value
        source = target


def per_device(frames, class_index, surface_mask, effusivity, conductivity):
    rows = lax.axis_size("row")
    cols = lax.axis_size("col")
    local, height, width = frames.shape
    tile_rows, tile_cols = height // rows, width // cols
    total = local * rows * cols
    if rows % 2 or local % 8 or tile_rows % GROUP or tile_cols != LANES or total % LANES or (local * cols) % LANES:
        return plain_device(frames, class_index, surface_mask, effusivity, conductivity)
    high_rows, wide_cols = tile_rows + 2 * PASSES, tile_cols + 2 * PAD
    vmem = pl.BlockSpec(memory_space=pltpu.VMEM)
    smem = pl.BlockSpec(memory_space=pltpu.SMEM)
    dma = pltpu.SemaphoreType.DMA
    sides = len(SIDES)
    flux, wide = pl.pallas_call(
        functools.partial(gather_kernel, rows, cols, tile_rows, tile_cols, local),
        out_shape=(
            jax.ShapeDtypeStruct((high_rows, wide_cols, total), jnp.float32),
            jax.ShapeDtypeStruct((high_rows, wide_cols, LANES), jnp.float32),
        ),
        in_specs=[pl.BlockSpec(memory_space=pltpu.HBM), vmem, vmem, smem, smem],
        out_specs=(vmem, vmem),
        scratch_shapes=[
            pltpu.VMEM((total, tile_rows, tile_cols), jnp.float32),
            pltpu.VMEM((2, tile_rows, tile_cols), jnp.float32),
            pltpu.VMEM((sides, 2, tile_rows, tile_cols), jnp.float32),
            pltpu.VMEM((high_rows, tile_cols, LANES), jnp.float32),
            pltpu.VMEM((2, total, total), jnp.bfloat16),
            pltpu.VMEM((2, PASSES, total, tile_cols), jnp.float32),
            pltpu.VMEM((2, PASSES, total, tile_cols), jnp.float32),
            pltpu.VMEM((total // 2, GROUP, tile_cols), jnp.float32),
            pltpu.VMEM((2, PASSES, high_rows, total), jnp.float32),
            pltpu.VMEM((2, PASSES, high_rows, total), jnp.float32),
            dma, dma((rows,)), dma, dma((sides,)), dma((sides,)),
            dma, dma((rows // 2,)), dma, dma((2, rows)), dma((2, rows)), dma((2,)), dma((2,)),
        ],
        compiler_params=pltpu.CompilerParams(
            collective_id=0, has_side_effects=True, vmem_limit_bytes=40 * 2**20
        ),
        name="gather",
    )(frames, class_index, surface_mask, effusivity, conductivity)
    return pl.pallas_call(
        relax_kernel,
        out_shape=jax.ShapeDtypeStruct((tile_rows, tile_cols, total), jnp.float32),
        grid=(total // LANES,),
        in_specs=[
            pl.BlockSpec((high_rows, wide_cols, LANES), lambda n: (0, 0, n)),
            pl.BlockSpec((high_rows, wide_cols, LANES), lambda n: (0, 0, 0)),
        ],
        out_specs=pl.BlockSpec((tile_rows, tile_cols, LANES), lambda n: (0, 0, n)),
        scratch_shapes=[pltpu.VMEM((high_rows, wide_cols, LANES), jnp.float32)] * 2,
        compiler_params=pltpu.CompilerParams(vmem_limit_bytes=24 * 2**20),
        name="relax",
    )(flux, wide)


def solution(mesh):
    in_specs = (P(("row", "col"), None, None), P("row", "col"), P("row", "col"), P(), P())
    out_specs = P("row", "col", None)
    return jax.shard_map(
        per_device, mesh=mesh, in_specs=in_specs, out_specs=out_specs, check_vma=False
    )
```

```python
import functools
import jax
import jax.numpy as jnp
from jax import lax
from jax.experimental import pallas as pl
from jax.experimental.pallas import tpu as pltpu
from jax.sharding import PartitionSpec as P

PASSES = 3
PAD = 8
GROUP = 8
LANES = 128
VMEM_GATHER = 40 * 2**20
MESH = pl.DeviceIdType.MESH

flux_factor = 1.1283791670955126
lateral_rate = 0.24


def extended(block, sides, width):
    for axis, dim in sides:
        count = lax.axis_size(axis)
        forward = [(i, i + 1) for i in range(count - 1)]
        backward = [(target, source) for source, target in forward]
        low = lax.ppermute(
            lax.slice_in_dim(block, block.shape[dim] - width, None, axis=dim), axis, forward
        )
        high = lax.ppermute(lax.slice_in_dim(block, 0, width, axis=dim), axis, backward)
        block = jnp.concatenate([low, block, high], axis=dim)
    return block


def weights(lagged):
    clipped = jnp.maximum(lagged, 0.0)
    return jnp.where(lagged >= 0.0, 1.0 / (jnp.sqrt(clipped) + jnp.sqrt(clipped + 1.0)), 0.0)


def kernel_from(later, earlier):
    lagged = (later[:, None] - earlier[None, :]).astype(jnp.float32)
    return weights(lagged) - weights(lagged - 1.0)


def relax_once(padded, lateral):
    center = padded[1:-1, 1:-1]
    laplace = (
        padded[2:, 1:-1] + padded[:-2, 1:-1] + padded[1:-1, 2:] + padded[1:-1, :-2] - 4.0 * center
    )
    return center + lateral[:, :, None] * laplace


def plain_device(frames, class_index, surface_mask, effusivity, conductivity):
    row_count = lax.axis_size("row")
    col_count = lax.axis_size("col")
    local_frames, height, width = frames.shape
    tile_rows = height // row_count
    tile_cols = width // col_count
    total_frames = local_frames * row_count * col_count
    frame_ids = jnp.arange(total_frames, dtype=jnp.int32)
    contract = (((0,), (1,)), ((), ()))
    kernel = kernel_from(frame_ids, frame_ids)
    blocks = frames.reshape(local_frames, row_count, tile_rows, col_count, tile_cols)
    blocks = blocks.transpose(0, 1, 3, 2, 4).reshape(
        local_frames, row_count * col_count, tile_rows, tile_cols
    )
    convolved = lax.dot_general(
        lax.all_to_all(blocks, ("row", "col"), split_axis=1, concat_axis=0, tiled=True)[:, 0],
        kernel,
        contract,
        precision=lax.Precision.HIGHEST,
    )
    classes = jnp.arange(effusivity.shape[0], dtype=jnp.int32)
    matches = (class_index[:, :, None] == classes[None, None, :]).astype(jnp.float32)
    maskf = surface_mask.astype(jnp.float32)
    gain = flux_factor * jnp.sum(matches * effusivity, axis=-1) * maskf
    lateral = lateral_rate * jnp.sum(matches * conductivity, axis=-1) * maskf
    heat_flux = convolved * gain[:, :, None]
    padded = extended(heat_flux, (("row", 0), ("col", 1)), PASSES)
    lateral_wide = extended(lateral, (("row", 0), ("col", 1)), PASSES - 1)
    for pass_index in range(PASSES):
        margin = PASSES - 1 - pass_index
        offset = PASSES - 1 - margin
        lateral_part = lateral_wide[
            offset : offset + tile_rows + 2 * margin, offset : offset + tile_cols + 2 * margin
        ]
        padded = relax_once(padded, lateral_part)
    return padded


SIDES = ((-1, 0), (1, 0), (0, -1), (0, 1), (-1, -1), (-1, 1), (1, -1), (1, 1))


def gather_kernel(
    rows, cols, tile_rows, tile_cols, local,
    frames, class_ref, mask_ref, eff_ref, cond_ref,
    flux, wide,
    held, lat, near, gain, mix_ref, edge, rim, strip, side_out, side_in,
    send_sem, recv_sem, own_sem, lat_send, lat_recv,
    strip_send, strip_recv, strip_own, relay_send, relay_recv, side_send, side_recv,
):
    row, col = lax.axis_index("row"), lax.axis_index("col")
    group = cols * local
    total = rows * group
    halo = PASSES
    chunks = total // LANES
    mid = rows // 2
    half = row // mid

    def there(step, count, at):
        return (at + step >= 0) & (at + step < count)

    def exists(side):
        return there(side[0], rows, row) & there(side[1], cols, col)

    classes = class_ref[...]
    maskf = mask_ref[...].astype(jnp.float32)
    eff = jnp.zeros(classes.shape, jnp.float32)
    cond = jnp.zeros(classes.shape, jnp.float32)
    for k in range(eff_ref.shape[0]):
        eff = jnp.where(classes == k, eff_ref[k], eff)
        cond = jnp.where(classes == k, cond_ref[k], cond)
    gain_rows = flux_factor * eff * maskf
    lat_rows = lateral_rate * cond * maskf
    lat[0] = lat_rows
    lat[1] = gain_rows
    near[...] = jnp.zeros_like(near)

    @pl.loop(0, tile_rows + 2 * halo)
    def _(h):
        for c in range(chunks):
            flux[c, h] = jnp.zeros(flux.shape[2:], jnp.float32)

    barrier = pltpu.get_barrier_semaphore()
    for k in range(rows):
        @pl.loop(0 if k else 1, cols)
        def _(j, k=k):
            pl.semaphore_signal(
                barrier, inc=1,
                device_id=(lax.rem(row + k, rows), lax.rem(col + j, cols)),
                device_id_type=MESH,
            )
    pl.semaphore_wait(barrier, rows * cols - 1)

    def lat_copy(i):
        side = SIDES[i]
        return pltpu.make_async_remote_copy(
            src_ref=lat, dst_ref=near.at[i], send_sem=lat_send.at[i], recv_sem=lat_recv.at[i],
            device_id=(row + side[0], col + side[1]), device_id_type=MESH,
        )

    def column(at):
        return pl.ds(pl.multiple_of(at * tile_cols, tile_cols), tile_cols)

    own = pltpu.make_async_copy(
        frames.at[:, pl.ds(pl.multiple_of(row * tile_rows, tile_rows), tile_rows), column(col)],
        held.at[pl.ds((row * cols + col) * local, local)],
        own_sem,
    )
    own.start()

    strip_row = mid - 1 + half
    strip_from = pl.ds(pl.multiple_of(mid * tile_rows - GROUP * half, GROUP), GROUP)
    strip_at = strip.at[pl.ds(((row - half * mid) * cols + col) * local, local)]
    beside = row == strip_row

    def strip_copy(j):
        to_col = lax.rem(col + j, cols)
        return pltpu.make_async_remote_copy(
            src_ref=frames.at[:, strip_from, column(to_col)], dst_ref=strip_at,
            send_sem=strip_send, recv_sem=strip_recv.at[row - half * mid],
            device_id=(strip_row, to_col), device_id_type=MESH,
        )

    strip_self = pltpu.make_async_copy(frames.at[:, strip_from, column(col)], strip_at, strip_own)

    def start_strips():
        @pl.loop(1, cols)
        def _(j):
            strip_copy(j).start()

        @pl.when(beside)
        def _():
            strip_self.start()

        @pl.when(jnp.logical_not(beside))
        def _():
            strip_copy(0).start()

    order = [2, 0, 1, 3]
    for k in order:
        @pl.loop(0 if k else 1, cols)
        def _(j, k=k):
            to_row, to_col = lax.rem(row + k, rows), lax.rem(col + j, cols)
            pltpu.make_async_remote_copy(
                src_ref=frames.at[
                    :, pl.ds(pl.multiple_of(to_row * tile_rows, tile_rows), tile_rows), column(to_col)
                ],
                dst_ref=held.at[pl.ds((row * cols + col) * local, local)],
                send_sem=send_sem, recv_sem=recv_sem.at[k],
                device_id=(to_row, to_col), device_id_type=MESH,
            ).start()
        if k == 0:
            start_strips()
        if k == order[0]:
            for i, side in enumerate(SIDES):
                @pl.when(exists(side))
                def _(i=i):
                    lat_copy(i).start()
    for k in range(rows):
        shape = (group, total)
        earlier = lax.broadcasted_iota(jnp.int32, shape, 0) + k * group
        later = lax.broadcasted_iota(jnp.int32, shape, 1)
        lagged = (later - earlier).astype(jnp.float32)
        mix = weights(lagged) - weights(lagged - 1.0)
        high = mix.astype(jnp.bfloat16)
        mix_ref[0, k * group : (k + 1) * group] = high
        mix_ref[1, k * group : (k + 1) * group] = (mix - high.astype(jnp.float32)).astype(jnp.bfloat16)

    def upright(line):
        return jnp.transpose(jnp.broadcast_to(line, (tile_cols, tile_cols)))[:, :LANES]

    for i, side in enumerate(SIDES):
        @pl.when(exists((-side[0], -side[1])))
        def _(i=i):
            lat_copy(i).wait_recv()
        @pl.when(exists(side))
        def _(i=i):
            lat_copy(i).wait_send()
    slot = {(-a, -b): i for i, (a, b) in enumerate(SIDES)}
    inside = slice(PAD, PAD + tile_cols)
    for h in range(-halo, tile_rows + halo):
        up = -1 if h < 0 else (1 if h >= tile_rows else 0)
        at = h - up * tile_rows
        def line(side, which=0):
            if side == (0, 0):
                return lat[which, at : at + 1, :]
            return near[slot[side], which, at : at + 1, :]
        wide[h + halo, inside] = upright(line((up, 0)))
        wide[h + halo, 0:PAD] = upright(line((up, -1)))[tile_cols - PAD :]
        wide[h + halo, PAD + tile_cols :] = upright(line((up, 1)))[:PAD]
        gain[h + halo] = upright(line((up, 0), 1))

    def frames_of(source):
        return pl.ds(pl.multiple_of(source * group, group), group)

    def product(x, source):
        count = x.shape[0]
        x = jnp.transpose(x, (0, 2, 1)).reshape(count * tile_cols, group)
        high = x.astype(jnp.bfloat16)
        low = (x - high.astype(jnp.float32)).astype(jnp.bfloat16)
        at = frames_of(source)
        out = jnp.dot(high, mix_ref[0, at], preferred_element_type=jnp.float32)
        out += jnp.dot(low, mix_ref[0, at], preferred_element_type=jnp.float32)
        out += jnp.dot(high, mix_ref[1, at], preferred_element_type=jnp.float32)
        return out.reshape(count, tile_cols, total)

    def wait_for(ref, sem):
        pltpu.make_async_copy(ref, ref, sem).wait()

    def relayed(side, at_row, source):
        if side == 0:
            return (at_row >= 1) & jnp.logical_not((at_row == mid) & (source < mid))
        return (at_row < rows - 1) & jnp.logical_not((at_row == mid - 1) & (source >= mid))

    def relay_copy(side, k):
        source = lax.rem(row - k + rows, rows)
        at = frames_of(source)
        return pltpu.make_async_remote_copy(
            src_ref=edge.at[side, :, at], dst_ref=rim.at[1 - side, :, at],
            send_sem=relay_send.at[side, k], recv_sem=relay_recv.at[1 - side, k],
            device_id=(row + (1 if side else -1), col), device_id_type=MESH,
        )

    def add(here, out, finish):
        for c in range(chunks):
            value = flux[c, here, inside] + out[:, :, c * LANES : (c + 1) * LANES]
            flux[c, here, inside] = value * gain[here] if finish else value

    last = tile_rows // GROUP - 1

    def main_part(k, finish):
        source = lax.rem(row - k + rows, rows)
        if k == 0:
            own.wait()
            wait_for(held.at[pl.ds(0, group - local)], recv_sem.at[k])
        else:
            wait_for(held.at[pl.ds(0, group)], recv_sem.at[k])
        at = frames_of(source)
        for q in range(last + 1):
            x = jnp.swapaxes(held[at, q * GROUP : (q + 1) * GROUP, :], 0, 1)
            if q == 0:
                edge[0, :, at] = x[:halo]
            if q == last:
                edge[1, :, at] = x[GROUP - halo :]
        for side in range(2):
            @pl.when(relayed(side, row, source))
            def _(side=side):
                relay_copy(side, k).start()
        for q in range(last + 1):
            x = jnp.swapaxes(held[at, q * GROUP : (q + 1) * GROUP, :], 0, 1)
            here = slice(halo + q * GROUP, halo + (q + 1) * GROUP)
            add(here, product(x, source), finish)

    def halo_part(k, finish):
        for side in range(2):
            beyond = row + (1 if side else -1)
            source = lax.rem(beyond - k + rows, rows)
            at = frames_of(source)
            here = slice(halo + tile_rows, 2 * halo + tile_rows) if side else slice(0, halo)

            @pl.when(there(1 if side else -1, rows, row))
            def _(side=side, beyond=beyond, source=source, at=at, here=here):
                direct = jnp.logical_not(relayed(1 - side, beyond, source))

                @pl.when(direct)
                def _():
                    turn = source - half * mid

                    @pl.when(source == row)
                    def _():
                        strip_self.wait()
                        wait_for(strip.at[pl.ds(0, group - local)], strip_recv.at[turn])

                    @pl.when(source != row)
                    def _():
                        wait_for(strip.at[pl.ds(0, group)], strip_recv.at[turn])

                    x = jnp.swapaxes(strip[frames_of(turn)], 0, 1)
                    rim[side, :, at] = x[:halo] if side else x[GROUP - halo :]

                @pl.when(jnp.logical_not(direct))
                def _():
                    wait_for(rim.at[side, :, at], relay_recv.at[side, k])

                add(here, product(rim[side, :, at], source), finish)

    visits = [2, 0, 1, 3]
    for k in visits[:-1]:
        main_part(k, False)
    for k in visits[:-2]:
        halo_part(k, False)
    main_part(visits[-1], True)
    halo_part(visits[-2], False)
    halo_part(visits[-1], True)

    def side_copy(i):
        return pltpu.make_async_remote_copy(
            src_ref=side_out.at[i], dst_ref=side_in.at[1 - i],
            send_sem=side_send.at[i], recv_sem=side_recv.at[1 - i],
            device_id=(row, col + (1 if i else -1)), device_id_type=MESH,
        )

    for i in range(2):
        for j in range(halo):
            at = PAD + j + (tile_cols - halo if i else 0)
            for c in range(chunks):
                side_out[i, j, c] = flux[c, :, at, :]
    for i in range(2):
        @pl.when(there(1 if i else -1, cols, col))
        def _(i=i):
            side_copy(i).start()

    wait_for(held.at[pl.ds(0, total - local)], send_sem)

    @pl.when(beside)
    def _():
        wait_for(strip.at[pl.ds(0, group - local)], strip_send)

    @pl.when(jnp.logical_not(beside))
    def _():
        wait_for(strip.at[pl.ds(0, group)], strip_send)

    for k in range(rows):
        for side in range(2):
            @pl.when(relayed(side, row, lax.rem(row - k + rows, rows)))
            def _(side=side, k=k):
                relay_copy(side, k).wait_send()
    for i in range(2):
        @pl.when(there(1 if i else -1, cols, col))
        def _(i=i):
            side_copy(i).wait_send()
            wait_for(side_in.at[i], side_recv.at[i])
            for j in range(halo):
                at = PAD + tile_cols + j if i else PAD - halo + j
                for c in range(chunks):
                    flux[c, :, at, :] = side_in[i, j, c]


def relax_kernel(flux, wide, out, first, second, third, sem):
    chunks, count, width = flux.shape[0], flux.shape[1], flux.shape[2]

    def out_copy(c):
        return pltpu.make_async_copy(
            third.at[c], out.at[:, :, c * LANES : (c + 1) * LANES], sem.at[c]
        )

    for c in range(chunks):
        source = flux.at[c]
        for step, target in enumerate((first, second, None)):
            a, b = (1 + step, width - 1 - step) if target is not None else (PAD, width - PAD)
            for h in range(step + 1, count - step - 1):
                center = source[h, a:b, :]
                laplace = (
                    source[h + 1, a:b, :] + source[h - 1, a:b, :]
                    + source[h, a + 1 : b + 1, :] + source[h, a - 1 : b - 1, :] - 4.0 * center
                )
                value = center + wide[h, a:b, :] * laplace
                if target is None:
                    third[c, h - PASSES] = value
                else:
                    target[h, a:b, :] = value
            source = target
        out_copy(c).start()
    for c in range(chunks):
        out_copy(c).wait()


def per_device(frames, class_index, surface_mask, effusivity, conductivity):
    rows = lax.axis_size("row")
    cols = lax.axis_size("col")
    local, height, width = frames.shape
    tile_rows, tile_cols = height // rows, width // cols
    total = local * rows * cols
    if rows % 2 or local % 8 or tile_rows % GROUP or tile_cols != LANES or total % LANES or (local * cols) % LANES:
        return plain_device(frames, class_index, surface_mask, effusivity, conductivity)
    chunks = total // LANES
    high_rows, wide_cols = tile_rows + 2 * PASSES, tile_cols + 2 * PAD
    vmem = pl.BlockSpec(memory_space=pltpu.VMEM)
    smem = pl.BlockSpec(memory_space=pltpu.SMEM)
    dma = pltpu.SemaphoreType.DMA
    sides = len(SIDES)
    arguments = (frames, class_index, surface_mask, effusivity, conductivity)
    flux, wide = pl.pallas_call(
        functools.partial(gather_kernel, rows, cols, tile_rows, tile_cols, local),
        out_shape=(
            jax.ShapeDtypeStruct((chunks, high_rows, wide_cols, LANES), jnp.float32),
            jax.ShapeDtypeStruct((high_rows, wide_cols, LANES), jnp.float32),
        ),
        in_specs=[pl.BlockSpec(memory_space=pltpu.HBM), vmem, vmem, smem, smem],
        out_specs=(vmem, vmem),
        scratch_shapes=[
            pltpu.VMEM((total, tile_rows, tile_cols), jnp.float32),
            pltpu.VMEM((2, tile_rows, tile_cols), jnp.float32),
            pltpu.VMEM((sides, 2, tile_rows, tile_cols), jnp.float32),
            pltpu.VMEM((high_rows, tile_cols, LANES), jnp.float32),
            pltpu.VMEM((2, total, total), jnp.bfloat16),
            pltpu.VMEM((2, PASSES, total, tile_cols), jnp.float32),
            pltpu.VMEM((2, PASSES, total, tile_cols), jnp.float32),
            pltpu.VMEM((total // 2, GROUP, tile_cols), jnp.float32),
            pltpu.VMEM((2, PASSES, chunks, high_rows, LANES), jnp.float32),
            pltpu.VMEM((2, PASSES, chunks, high_rows, LANES), jnp.float32),
            dma, dma((rows,)), dma, dma((sides,)), dma((sides,)),
            dma, dma((rows // 2,)), dma, dma((2, rows)), dma((2, rows)), dma((2,)), dma((2,)),
        ],
        compiler_params=pltpu.CompilerParams(
            collective_id=0, has_side_effects=True, vmem_limit_bytes=VMEM_GATHER
        ),
        name="gather",
    )(*(pltpu.with_memory_space_constraint(x, pltpu.HBM) for x in arguments))
    return pl.pallas_call(
        relax_kernel,
        out_shape=jax.ShapeDtypeStruct((tile_rows, tile_cols, total), jnp.float32),
        in_specs=[vmem, vmem],
        out_specs=pl.BlockSpec(memory_space=pltpu.HBM),
        scratch_shapes=[pltpu.VMEM((high_rows, wide_cols, LANES), jnp.float32)] * 2
        + [pltpu.VMEM((chunks, tile_rows, tile_cols, LANES), jnp.float32), dma((chunks,))],
        compiler_params=pltpu.CompilerParams(vmem_limit_bytes=24 * 2**20),
        name="relax",
    )(flux, wide)


def solution(mesh):
    in_specs = (P(("row", "col"), None, None), P("row", "col"), P("row", "col"), P(), P())
    out_specs = P("row", "col", None)
    return jax.shard_map(
        per_device, mesh=mesh, in_specs=in_specs, out_specs=out_specs, check_vma=False
    )
```

```python
import functools
import jax
import jax.numpy as jnp
from jax import lax
from jax.experimental import pallas as pl
from jax.experimental.pallas import tpu as pltpu
from jax.sharding import PartitionSpec as P

PASSES = 3
PAD = 8
GROUP = 8
LANES = 128
VMEM_GATHER = 40 * 2**20
MESH = pl.DeviceIdType.MESH

flux_factor = 1.1283791670955126
lateral_rate = 0.24


def extended(block, sides, width):
    for axis, dim in sides:
        count = lax.axis_size(axis)
        forward = [(i, i + 1) for i in range(count - 1)]
        backward = [(target, source) for source, target in forward]
        low = lax.ppermute(
            lax.slice_in_dim(block, block.shape[dim] - width, None, axis=dim), axis, forward
        )
        high = lax.ppermute(lax.slice_in_dim(block, 0, width, axis=dim), axis, backward)
        block = jnp.concatenate([low, block, high], axis=dim)
    return block


def weights(lagged):
    clipped = jnp.maximum(lagged, 0.0)
    return jnp.where(lagged >= 0.0, 1.0 / (jnp.sqrt(clipped) + jnp.sqrt(clipped + 1.0)), 0.0)


def kernel_from(later, earlier):
    lagged = (later[:, None] - earlier[None, :]).astype(jnp.float32)
    return weights(lagged) - weights(lagged - 1.0)


def relax_once(padded, lateral):
    center = padded[1:-1, 1:-1]
    laplace = (
        padded[2:, 1:-1] + padded[:-2, 1:-1] + padded[1:-1, 2:] + padded[1:-1, :-2] - 4.0 * center
    )
    return center + lateral[:, :, None] * laplace


def plain_device(frames, class_index, surface_mask, effusivity, conductivity):
    row_count = lax.axis_size("row")
    col_count = lax.axis_size("col")
    local_frames, height, width = frames.shape
    tile_rows = height // row_count
    tile_cols = width // col_count
    total_frames = local_frames * row_count * col_count
    frame_ids = jnp.arange(total_frames, dtype=jnp.int32)
    contract = (((0,), (1,)), ((), ()))
    kernel = kernel_from(frame_ids, frame_ids)
    blocks = frames.reshape(local_frames, row_count, tile_rows, col_count, tile_cols)
    blocks = blocks.transpose(0, 1, 3, 2, 4).reshape(
        local_frames, row_count * col_count, tile_rows, tile_cols
    )
    convolved = lax.dot_general(
        lax.all_to_all(blocks, ("row", "col"), split_axis=1, concat_axis=0, tiled=True)[:, 0],
        kernel,
        contract,
        precision=lax.Precision.HIGHEST,
    )
    classes = jnp.arange(effusivity.shape[0], dtype=jnp.int32)
    matches = (class_index[:, :, None] == classes[None, None, :]).astype(jnp.float32)
    maskf = surface_mask.astype(jnp.float32)
    gain = flux_factor * jnp.sum(matches * effusivity, axis=-1) * maskf
    lateral = lateral_rate * jnp.sum(matches * conductivity, axis=-1) * maskf
    heat_flux = convolved * gain[:, :, None]
    padded = extended(heat_flux, (("row", 0), ("col", 1)), PASSES)
    lateral_wide = extended(lateral, (("row", 0), ("col", 1)), PASSES - 1)
    for pass_index in range(PASSES):
        margin = PASSES - 1 - pass_index
        offset = PASSES - 1 - margin
        lateral_part = lateral_wide[
            offset : offset + tile_rows + 2 * margin, offset : offset + tile_cols + 2 * margin
        ]
        padded = relax_once(padded, lateral_part)
    return padded


SIDES = ((-1, 0), (1, 0), (0, -1), (0, 1), (-1, -1), (-1, 1), (1, -1), (1, 1))


def gather_kernel(
    rows, cols, tile_rows, tile_cols, local,
    frames, class_ref, mask_ref, eff_ref, cond_ref,
    flux, wide,
    held, lat, near, gain, mix_ref, edge, rim, strip, side_out, side_in,
    send_sem, recv_sem, own_sem, lat_send, lat_recv,
    strip_send, strip_recv, strip_own, relay_send, relay_recv, side_send, side_recv,
):
    row, col = lax.axis_index("row"), lax.axis_index("col")
    group = cols * local
    total = rows * group
    halo = PASSES
    chunks = total // LANES
    mid = rows // 2
    half = row // mid

    def there(step, count, at):
        return (at + step >= 0) & (at + step < count)

    def exists(side):
        return there(side[0], rows, row) & there(side[1], cols, col)

    classes = class_ref[...]
    maskf = mask_ref[...].astype(jnp.float32)
    eff = jnp.zeros(classes.shape, jnp.float32)
    cond = jnp.zeros(classes.shape, jnp.float32)
    for k in range(eff_ref.shape[0]):
        eff = jnp.where(classes == k, eff_ref[k], eff)
        cond = jnp.where(classes == k, cond_ref[k], cond)
    gain_rows = flux_factor * eff * maskf
    lat_rows = lateral_rate * cond * maskf
    lat[0] = lat_rows
    lat[1] = gain_rows
    near[...] = jnp.zeros_like(near)

    @pl.loop(0, tile_rows + 2 * halo)
    def _(h):
        for c in range(chunks):
            flux[c, h] = jnp.zeros(flux.shape[2:], jnp.float32)

    barrier = pltpu.get_barrier_semaphore()
    for k in range(rows):
        @pl.loop(0 if k else 1, cols)
        def _(j, k=k):
            pl.semaphore_signal(
                barrier, inc=1,
                device_id=(lax.rem(row + k, rows), lax.rem(col + j, cols)),
                device_id_type=MESH,
            )
    pl.semaphore_wait(barrier, rows * cols - 1)

    def lat_copy(i):
        side = SIDES[i]
        return pltpu.make_async_remote_copy(
            src_ref=lat, dst_ref=near.at[i], send_sem=lat_send.at[i], recv_sem=lat_recv.at[i],
            device_id=(row + side[0], col + side[1]), device_id_type=MESH,
        )

    def column(at):
        return pl.ds(pl.multiple_of(at * tile_cols, tile_cols), tile_cols)

    own = pltpu.make_async_copy(
        frames.at[:, pl.ds(pl.multiple_of(row * tile_rows, tile_rows), tile_rows), column(col)],
        held.at[pl.ds((row * cols + col) * local, local)],
        own_sem,
    )
    own.start()

    strip_row = mid - 1 + half
    strip_from = pl.ds(pl.multiple_of(mid * tile_rows - GROUP * half, GROUP), GROUP)
    strip_at = strip.at[pl.ds(((row - half * mid) * cols + col) * local, local)]
    beside = row == strip_row

    def strip_copy(j):
        to_col = lax.rem(col + j, cols)
        return pltpu.make_async_remote_copy(
            src_ref=frames.at[:, strip_from, column(to_col)], dst_ref=strip_at,
            send_sem=strip_send, recv_sem=strip_recv.at[row - half * mid],
            device_id=(strip_row, to_col), device_id_type=MESH,
        )

    strip_self = pltpu.make_async_copy(frames.at[:, strip_from, column(col)], strip_at, strip_own)

    def start_strips():
        @pl.loop(1, cols)
        def _(j):
            strip_copy(j).start()

        @pl.when(beside)
        def _():
            strip_self.start()

        @pl.when(jnp.logical_not(beside))
        def _():
            strip_copy(0).start()

    order = [mid, 0] + [k for k in range(1, rows) if k != mid]
    for k in order:
        @pl.loop(0 if k else 1, cols)
        def _(j, k=k):
            to_row, to_col = lax.rem(row + k, rows), lax.rem(col + j, cols)
            pltpu.make_async_remote_copy(
                src_ref=frames.at[
                    :, pl.ds(pl.multiple_of(to_row * tile_rows, tile_rows), tile_rows), column(to_col)
                ],
                dst_ref=held.at[pl.ds((row * cols + col) * local, local)],
                send_sem=send_sem, recv_sem=recv_sem.at[k],
                device_id=(to_row, to_col), device_id_type=MESH,
            ).start()
        if k == 0:
            start_strips()
        if k == order[0]:
            for i, side in enumerate(SIDES):
                @pl.when(exists(side))
                def _(i=i):
                    lat_copy(i).start()
    for k in range(rows):
        shape = (group, total)
        earlier = lax.broadcasted_iota(jnp.int32, shape, 0) + k * group
        later = lax.broadcasted_iota(jnp.int32, shape, 1)
        lagged = (later - earlier).astype(jnp.float32)
        mix = weights(lagged) - weights(lagged - 1.0)
        high = mix.astype(jnp.bfloat16)
        mix_ref[0, k * group : (k + 1) * group] = high
        mix_ref[1, k * group : (k + 1) * group] = (mix - high.astype(jnp.float32)).astype(jnp.bfloat16)

    def upright(line):
        return jnp.transpose(jnp.broadcast_to(line, (tile_cols, tile_cols)))[:, :LANES]

    for i, side in enumerate(SIDES):
        @pl.when(exists((-side[0], -side[1])))
        def _(i=i):
            lat_copy(i).wait_recv()
        @pl.when(exists(side))
        def _(i=i):
            lat_copy(i).wait_send()
    slot = {(-a, -b): i for i, (a, b) in enumerate(SIDES)}
    inside = slice(PAD, PAD + tile_cols)
    for h in range(-halo, tile_rows + halo):
        up = -1 if h < 0 else (1 if h >= tile_rows else 0)
        at = h - up * tile_rows
        def line(side, which=0):
            if side == (0, 0):
                return lat[which, at : at + 1, :]
            return near[slot[side], which, at : at + 1, :]
        wide[h + halo, inside] = upright(line((up, 0)))
        wide[h + halo, 0:PAD] = upright(line((up, -1)))[tile_cols - PAD :]
        wide[h + halo, PAD + tile_cols :] = upright(line((up, 1)))[:PAD]
        gain[h + halo] = upright(line((up, 0), 1))

    def frames_of(source):
        return pl.ds(pl.multiple_of(source * group, group), group)

    def product(x, source):
        count = x.shape[0]
        x = jnp.transpose(x, (0, 2, 1)).reshape(count * tile_cols, group)
        high = x.astype(jnp.bfloat16)
        low = (x - high.astype(jnp.float32)).astype(jnp.bfloat16)
        at = frames_of(source)
        out = jnp.dot(high, mix_ref[0, at], preferred_element_type=jnp.float32)
        out += jnp.dot(low, mix_ref[0, at], preferred_element_type=jnp.float32)
        out += jnp.dot(high, mix_ref[1, at], preferred_element_type=jnp.float32)
        return out.reshape(count, tile_cols, total)

    def wait_for(ref, sem):
        pltpu.make_async_copy(ref, ref, sem).wait()

    def relayed(side, at_row, source):
        if side == 0:
            return (at_row >= 1) & jnp.logical_not((at_row == mid) & (source < mid))
        return (at_row < rows - 1) & jnp.logical_not((at_row == mid - 1) & (source >= mid))

    def relay_copy(side, k):
        source = lax.rem(row - k + rows, rows)
        at = frames_of(source)
        return pltpu.make_async_remote_copy(
            src_ref=edge.at[side, :, at], dst_ref=rim.at[1 - side, :, at],
            send_sem=relay_send.at[side, k], recv_sem=relay_recv.at[1 - side, k],
            device_id=(row + (1 if side else -1), col), device_id_type=MESH,
        )

    def add(here, out, finish):
        for c in range(chunks):
            value = flux[c, here, inside] + out[:, :, c * LANES : (c + 1) * LANES]
            flux[c, here, inside] = value * gain[here] if finish else value

    last = tile_rows // GROUP - 1

    def main_part(k, finish):
        source = lax.rem(row - k + rows, rows)
        if k == 0:
            own.wait()
            wait_for(held.at[pl.ds(0, group - local)], recv_sem.at[k])
        else:
            wait_for(held.at[pl.ds(0, group)], recv_sem.at[k])
        at = frames_of(source)
        for q in range(last + 1):
            x = jnp.swapaxes(held[at, q * GROUP : (q + 1) * GROUP, :], 0, 1)
            if q == 0:
                edge[0, :, at] = x[:halo]
            if q == last:
                edge[1, :, at] = x[GROUP - halo :]
        for side in range(2):
            @pl.when(relayed(side, row, source))
            def _(side=side):
                relay_copy(side, k).start()
        for q in range(last + 1):
            x = jnp.swapaxes(held[at, q * GROUP : (q + 1) * GROUP, :], 0, 1)
            here = slice(halo + q * GROUP, halo + (q + 1) * GROUP)
            add(here, product(x, source), finish)

    def halo_part(k, finish):
        for side in range(2):
            beyond = row + (1 if side else -1)
            source = lax.rem(beyond - k + rows, rows)
            at = frames_of(source)
            here = slice(halo + tile_rows, 2 * halo + tile_rows) if side else slice(0, halo)

            @pl.when(there(1 if side else -1, rows, row))
            def _(side=side, beyond=beyond, source=source, at=at, here=here):
                direct = jnp.logical_not(relayed(1 - side, beyond, source))

                @pl.when(direct)
                def _():
                    turn = source - half * mid

                    @pl.when(source == row)
                    def _():
                        strip_self.wait()
                        wait_for(strip.at[pl.ds(0, group - local)], strip_recv.at[turn])

                    @pl.when(source != row)
                    def _():
                        wait_for(strip.at[pl.ds(0, group)], strip_recv.at[turn])

                    x = jnp.swapaxes(strip[frames_of(turn)], 0, 1)
                    rim[side, :, at] = x[:halo] if side else x[GROUP - halo :]

                @pl.when(jnp.logical_not(direct))
                def _():
                    wait_for(rim.at[side, :, at], relay_recv.at[side, k])

                add(here, product(rim[side, :, at], source), finish)

    visits = order
    for k in visits[:-1]:
        main_part(k, False)
    for k in visits[:-2]:
        halo_part(k, False)
    main_part(visits[-1], True)
    halo_part(visits[-2], False)
    halo_part(visits[-1], True)

    def side_copy(i):
        return pltpu.make_async_remote_copy(
            src_ref=side_out.at[i], dst_ref=side_in.at[1 - i],
            send_sem=side_send.at[i], recv_sem=side_recv.at[1 - i],
            device_id=(row, col + (1 if i else -1)), device_id_type=MESH,
        )

    for i in range(2):
        for j in range(halo):
            at = PAD + j + (tile_cols - halo if i else 0)
            for c in range(chunks):
                side_out[i, j, c] = flux[c, :, at, :]
    for i in range(2):
        @pl.when(there(1 if i else -1, cols, col))
        def _(i=i):
            side_copy(i).start()

    wait_for(held.at[pl.ds(0, total - local)], send_sem)

    @pl.when(beside)
    def _():
        wait_for(strip.at[pl.ds(0, group - local)], strip_send)

    @pl.when(jnp.logical_not(beside))
    def _():
        wait_for(strip.at[pl.ds(0, group)], strip_send)

    for k in range(rows):
        for side in range(2):
            @pl.when(relayed(side, row, lax.rem(row - k + rows, rows)))
            def _(side=side, k=k):
                relay_copy(side, k).wait_send()
    for i in range(2):
        @pl.when(there(1 if i else -1, cols, col))
        def _(i=i):
            side_copy(i).wait_send()
            wait_for(side_in.at[i], side_recv.at[i])
            for j in range(halo):
                at = PAD + tile_cols + j if i else PAD - halo + j
                for c in range(chunks):
                    flux[c, :, at, :] = side_in[i, j, c]


def relax_kernel(flux, wide, out, first, second, third, sem):
    chunks, count, width = flux.shape[0], flux.shape[1], flux.shape[2]

    def out_copy(c):
        return pltpu.make_async_copy(
            third.at[c], out.at[:, :, c * LANES : (c + 1) * LANES], sem.at[c]
        )

    for c in range(chunks):
        source = flux.at[c]
        for step, target in enumerate((first, second, None)):
            if target is None:
                bounds = [PAD, PAD + (width - 2 * PAD) // 2, width - PAD]
            else:
                bounds = [1 + step, width // 2, width - 1 - step]
            for a, b in zip(bounds[:-1], bounds[1:]):
                above, center = source[step, a:b, :], source[step + 1, a:b, :]
                for h in range(step + 1, count - step - 1):
                    below = source[h + 1, a:b, :]
                    laplace = (
                        below + above
                        + source[h, a + 1 : b + 1, :] + source[h, a - 1 : b - 1, :] - 4.0 * center
                    )
                    value = center + wide[h, a:b, :] * laplace
                    if target is None:
                        third[c, h - PASSES, a - PAD : b - PAD] = value
                    else:
                        target[h, a:b, :] = value
                    above, center = center, below
            source = target
        out_copy(c).start()
    for c in range(chunks):
        out_copy(c).wait()


def per_device(frames, class_index, surface_mask, effusivity, conductivity):
    rows = lax.axis_size("row")
    cols = lax.axis_size("col")
    local, height, width = frames.shape
    tile_rows, tile_cols = height // rows, width // cols
    total = local * rows * cols
    if rows % 2 or local % 8 or tile_rows % GROUP or tile_cols != LANES or total % LANES or (local * cols) % LANES:
        return plain_device(frames, class_index, surface_mask, effusivity, conductivity)
    chunks = total // LANES
    high_rows, wide_cols = tile_rows + 2 * PASSES, tile_cols + 2 * PAD
    vmem = pl.BlockSpec(memory_space=pltpu.VMEM)
    smem = pl.BlockSpec(memory_space=pltpu.SMEM)
    dma = pltpu.SemaphoreType.DMA
    sides = len(SIDES)
    arguments = (frames, class_index, surface_mask, effusivity, conductivity)
    flux, wide = pl.pallas_call(
        functools.partial(gather_kernel, rows, cols, tile_rows, tile_cols, local),
        out_shape=(
            jax.ShapeDtypeStruct((chunks, high_rows, wide_cols, LANES), jnp.float32),
            jax.ShapeDtypeStruct((high_rows, wide_cols, LANES), jnp.float32),
        ),
        in_specs=[pl.BlockSpec(memory_space=pltpu.HBM), vmem, vmem, smem, smem],
        out_specs=(vmem, vmem),
        scratch_shapes=[
            pltpu.VMEM((total, tile_rows, tile_cols), jnp.float32),
            pltpu.VMEM((2, tile_rows, tile_cols), jnp.float32),
            pltpu.VMEM((sides, 2, tile_rows, tile_cols), jnp.float32),
            pltpu.VMEM((high_rows, tile_cols, LANES), jnp.float32),
            pltpu.VMEM((2, total, total), jnp.bfloat16),
            pltpu.VMEM((2, PASSES, total, tile_cols), jnp.float32),
            pltpu.VMEM((2, PASSES, total, tile_cols), jnp.float32),
            pltpu.VMEM((total // 2, GROUP, tile_cols), jnp.float32),
            pltpu.VMEM((2, PASSES, chunks, high_rows, LANES), jnp.float32),
            pltpu.VMEM((2, PASSES, chunks, high_rows, LANES), jnp.float32),
            dma, dma((rows,)), dma, dma((sides,)), dma((sides,)),
            dma, dma((rows // 2,)), dma, dma((2, rows)), dma((2, rows)), dma((2,)), dma((2,)),
        ],
        compiler_params=pltpu.CompilerParams(
            collective_id=0, has_side_effects=True, vmem_limit_bytes=VMEM_GATHER
        ),
        name="gather",
    )(*(pltpu.with_memory_space_constraint(x, pltpu.HBM) for x in arguments))
    return pl.pallas_call(
        relax_kernel,
        out_shape=jax.ShapeDtypeStruct((tile_rows, tile_cols, total), jnp.float32),
        in_specs=[vmem, vmem],
        out_specs=pl.BlockSpec(memory_space=pltpu.HBM),
        scratch_shapes=[pltpu.VMEM((high_rows, wide_cols, LANES), jnp.float32)] * 2
        + [pltpu.VMEM((chunks, tile_rows, tile_cols, LANES), jnp.float32), dma((chunks,))],
        compiler_params=pltpu.CompilerParams(vmem_limit_bytes=24 * 2**20),
        name="relax",
    )(flux, wide)


def solution(mesh):
    in_specs = (P(("row", "col"), None, None), P("row", "col"), P("row", "col"), P(), P())
    out_specs = P("row", "col", None)
    return jax.shard_map(
        per_device, mesh=mesh, in_specs=in_specs, out_specs=out_specs, check_vma=False
    )
```

```python
import functools
import jax
import jax.numpy as jnp
from jax import lax
from jax.experimental import pallas as pl
from jax.experimental.pallas import tpu as pltpu
from jax.sharding import PartitionSpec as P

PASSES = 3
PAD = 8
GROUP = 8
LANES = 128
VMEM_GATHER = 40 * 2**20
MESH = pl.DeviceIdType.MESH

flux_factor = 1.1283791670955126
lateral_rate = 0.24


def extended(block, sides, width):
    for axis, dim in sides:
        count = lax.axis_size(axis)
        forward = [(i, i + 1) for i in range(count - 1)]
        backward = [(target, source) for source, target in forward]
        low = lax.ppermute(
            lax.slice_in_dim(block, block.shape[dim] - width, None, axis=dim), axis, forward
        )
        high = lax.ppermute(lax.slice_in_dim(block, 0, width, axis=dim), axis, backward)
        block = jnp.concatenate([low, block, high], axis=dim)
    return block


def weights(lagged):
    clipped = jnp.maximum(lagged, 0.0)
    return jnp.where(lagged >= 0.0, 1.0 / (jnp.sqrt(clipped) + jnp.sqrt(clipped + 1.0)), 0.0)


def kernel_from(later, earlier):
    lagged = (later[:, None] - earlier[None, :]).astype(jnp.float32)
    return weights(lagged) - weights(lagged - 1.0)


def relax_once(padded, lateral):
    center = padded[1:-1, 1:-1]
    laplace = (
        padded[2:, 1:-1] + padded[:-2, 1:-1] + padded[1:-1, 2:] + padded[1:-1, :-2] - 4.0 * center
    )
    return center + lateral[:, :, None] * laplace


def plain_device(frames, class_index, surface_mask, effusivity, conductivity):
    row_count = lax.axis_size("row")
    col_count = lax.axis_size("col")
    local_frames, height, width = frames.shape
    tile_rows = height // row_count
    tile_cols = width // col_count
    total_frames = local_frames * row_count * col_count
    frame_ids = jnp.arange(total_frames, dtype=jnp.int32)
    contract = (((0,), (1,)), ((), ()))
    kernel = kernel_from(frame_ids, frame_ids)
    blocks = frames.reshape(local_frames, row_count, tile_rows, col_count, tile_cols)
    blocks = blocks.transpose(0, 1, 3, 2, 4).reshape(
        local_frames, row_count * col_count, tile_rows, tile_cols
    )
    convolved = lax.dot_general(
        lax.all_to_all(blocks, ("row", "col"), split_axis=1, concat_axis=0, tiled=True)[:, 0],
        kernel,
        contract,
        precision=lax.Precision.HIGHEST,
    )
    classes = jnp.arange(effusivity.shape[0], dtype=jnp.int32)
    matches = (class_index[:, :, None] == classes[None, None, :]).astype(jnp.float32)
    maskf = surface_mask.astype(jnp.float32)
    gain = flux_factor * jnp.sum(matches * effusivity, axis=-1) * maskf
    lateral = lateral_rate * jnp.sum(matches * conductivity, axis=-1) * maskf
    heat_flux = convolved * gain[:, :, None]
    padded = extended(heat_flux, (("row", 0), ("col", 1)), PASSES)
    lateral_wide = extended(lateral, (("row", 0), ("col", 1)), PASSES - 1)
    for pass_index in range(PASSES):
        margin = PASSES - 1 - pass_index
        offset = PASSES - 1 - margin
        lateral_part = lateral_wide[
            offset : offset + tile_rows + 2 * margin, offset : offset + tile_cols + 2 * margin
        ]
        padded = relax_once(padded, lateral_part)
    return padded


SIDES = ((-1, 0), (1, 0), (0, -1), (0, 1), (-1, -1), (-1, 1), (1, -1), (1, 1))


def gather_kernel(
    rows, cols, tile_rows, tile_cols, local,
    frames, class_ref, mask_ref, eff_ref, cond_ref,
    flux, wide,
    held, lat, near, gain, mix_ref, edge, rim, strip, side_out, side_in,
    send_sem, recv_sem, own_sem, lat_send, lat_recv,
    strip_send, strip_recv, strip_own, relay_send, relay_recv, side_send, side_recv,
):
    row, col = lax.axis_index("row"), lax.axis_index("col")
    group = cols * local
    total = rows * group
    halo = PASSES
    chunks = total // LANES
    mid = rows // 2
    half = row // mid

    def there(step, count, at):
        return (at + step >= 0) & (at + step < count)

    def exists(side):
        return there(side[0], rows, row) & there(side[1], cols, col)

    classes = class_ref[...]
    maskf = mask_ref[...].astype(jnp.float32)
    eff = jnp.zeros(classes.shape, jnp.float32)
    cond = jnp.zeros(classes.shape, jnp.float32)
    for k in range(eff_ref.shape[0]):
        eff = jnp.where(classes == k, eff_ref[k], eff)
        cond = jnp.where(classes == k, cond_ref[k], cond)
    gain_rows = flux_factor * eff * maskf
    lat_rows = lateral_rate * cond * maskf
    lat[0] = lat_rows
    lat[1] = gain_rows
    near[...] = jnp.zeros_like(near)

    @pl.loop(0, tile_rows + 2 * halo)
    def _(h):
        for c in range(chunks):
            flux[c, h] = jnp.zeros(flux.shape[2:], jnp.float32)

    barrier = pltpu.get_barrier_semaphore()
    for k in range(rows):
        @pl.loop(0 if k else 1, cols)
        def _(j, k=k):
            pl.semaphore_signal(
                barrier, inc=1,
                device_id=(lax.rem(row + k, rows), lax.rem(col + j, cols)),
                device_id_type=MESH,
            )
    pl.semaphore_wait(barrier, rows * cols - 1)

    def lat_copy(i):
        side = SIDES[i]
        return pltpu.make_async_remote_copy(
            src_ref=lat, dst_ref=near.at[i], send_sem=lat_send.at[i], recv_sem=lat_recv.at[i],
            device_id=(row + side[0], col + side[1]), device_id_type=MESH,
        )

    def column(at):
        return pl.ds(pl.multiple_of(at * tile_cols, tile_cols), tile_cols)

    own = pltpu.make_async_copy(
        frames.at[:, pl.ds(pl.multiple_of(row * tile_rows, tile_rows), tile_rows), column(col)],
        held.at[pl.ds((row * cols + col) * local, local)],
        own_sem,
    )
    own.start()

    strip_row = mid - 1 + half
    strip_from = pl.ds(pl.multiple_of(mid * tile_rows - GROUP * half, GROUP), GROUP)
    strip_at = strip.at[pl.ds(((row - half * mid) * cols + col) * local, local)]
    beside = row == strip_row

    def strip_copy(j):
        to_col = lax.rem(col + j, cols)
        return pltpu.make_async_remote_copy(
            src_ref=frames.at[:, strip_from, column(to_col)], dst_ref=strip_at,
            send_sem=strip_send, recv_sem=strip_recv.at[row - half * mid],
            device_id=(strip_row, to_col), device_id_type=MESH,
        )

    strip_self = pltpu.make_async_copy(frames.at[:, strip_from, column(col)], strip_at, strip_own)

    def start_strips():
        @pl.loop(1, cols)
        def _(j):
            strip_copy(j).start()

        @pl.when(beside)
        def _():
            strip_self.start()

        @pl.when(jnp.logical_not(beside))
        def _():
            strip_copy(0).start()

    order = [mid, 0] + [k for k in range(1, rows) if k != mid]
    final = order[-1]
    part_cols = cols // 2
    part = group // 2
    own_part = col // part_cols

    def send(k, to_col, sem):
        to_row = lax.rem(row + k, rows)
        pltpu.make_async_remote_copy(
            src_ref=frames.at[
                :, pl.ds(pl.multiple_of(to_row * tile_rows, tile_rows), tile_rows), column(to_col)
            ],
            dst_ref=held.at[pl.ds((row * cols + col) * local, local)],
            send_sem=send_sem, recv_sem=recv_sem.at[sem],
            device_id=(to_row, to_col), device_id_type=MESH,
        ).start()

    for k in order:
        if k and k == final:
            for turn in range(2):
                @pl.loop(0, part_cols)
                def _(j, k=k, turn=turn):
                    half_at = lax.rem(own_part + turn, 2) * part_cols
                    send(k, half_at + lax.rem(col + j, part_cols), rows if turn else k)
        else:
            @pl.loop(0 if k else 1, cols)
            def _(j, k=k):
                send(k, lax.rem(col + j, cols), k)
        if k == 0:
            start_strips()
        if k == order[0]:
            for i, side in enumerate(SIDES):
                @pl.when(exists(side))
                def _(i=i):
                    lat_copy(i).start()
    for k in range(rows):
        shape = (group, total)
        earlier = lax.broadcasted_iota(jnp.int32, shape, 0) + k * group
        later = lax.broadcasted_iota(jnp.int32, shape, 1)
        lagged = (later - earlier).astype(jnp.float32)
        mix = weights(lagged) - weights(lagged - 1.0)
        high = mix.astype(jnp.bfloat16)
        mix_ref[0, k * group : (k + 1) * group] = high
        mix_ref[1, k * group : (k + 1) * group] = (mix - high.astype(jnp.float32)).astype(jnp.bfloat16)

    def upright(line):
        return jnp.transpose(jnp.broadcast_to(line, (tile_cols, tile_cols)))[:, :LANES]

    for i, side in enumerate(SIDES):
        @pl.when(exists((-side[0], -side[1])))
        def _(i=i):
            lat_copy(i).wait_recv()
        @pl.when(exists(side))
        def _(i=i):
            lat_copy(i).wait_send()
    slot = {(-a, -b): i for i, (a, b) in enumerate(SIDES)}
    inside = slice(PAD, PAD + tile_cols)
    for h in range(-halo, tile_rows + halo):
        up = -1 if h < 0 else (1 if h >= tile_rows else 0)
        at = h - up * tile_rows
        def line(side, which=0):
            if side == (0, 0):
                return lat[which, at : at + 1, :]
            return near[slot[side], which, at : at + 1, :]
        wide[h + halo, inside] = upright(line((up, 0)))
        wide[h + halo, 0:PAD] = upright(line((up, -1)))[tile_cols - PAD :]
        wide[h + halo, PAD + tile_cols :] = upright(line((up, 1)))[:PAD]
        gain[h + halo] = upright(line((up, 0), 1))

    def frames_of(source):
        return pl.ds(pl.multiple_of(source * group, group), group)

    def piece(source, turn):
        if turn is None:
            return frames_of(source)
        which = lax.rem(own_part + turn, 2)
        return pl.ds(pl.multiple_of(source * group + which * part, part), part)

    def product(x, at):
        count = x.shape[0]
        x = jnp.transpose(x, (0, 2, 1)).reshape(count * tile_cols, x.shape[1])
        high = x.astype(jnp.bfloat16)
        low = (x - high.astype(jnp.float32)).astype(jnp.bfloat16)
        out = jnp.dot(high, mix_ref[0, at], preferred_element_type=jnp.float32)
        out += jnp.dot(low, mix_ref[0, at], preferred_element_type=jnp.float32)
        out += jnp.dot(high, mix_ref[1, at], preferred_element_type=jnp.float32)
        return out.reshape(count, tile_cols, total)

    def wait_for(ref, sem):
        pltpu.make_async_copy(ref, ref, sem).wait()

    def relayed(side, at_row, source):
        if side == 0:
            return (at_row >= 1) & jnp.logical_not((at_row == mid) & (source < mid))
        return (at_row < rows - 1) & jnp.logical_not((at_row == mid - 1) & (source >= mid))

    def relay_copy(side, k, turn=None):
        source = lax.rem(row - k + rows, rows)
        at = piece(source, turn)
        k = rows if turn else k
        return pltpu.make_async_remote_copy(
            src_ref=edge.at[side, :, at], dst_ref=rim.at[1 - side, :, at],
            send_sem=relay_send.at[side, k], recv_sem=relay_recv.at[1 - side, k],
            device_id=(row + (1 if side else -1), col), device_id_type=MESH,
        )

    def add(here, out, finish):
        for c in range(chunks):
            value = flux[c, here, inside] + out[:, :, c * LANES : (c + 1) * LANES]
            flux[c, here, inside] = value * gain[here] if finish else value

    last = tile_rows // GROUP - 1

    def main_part(k, finish, turn=None):
        source = lax.rem(row - k + rows, rows)
        if k == 0:
            own.wait()
            wait_for(held.at[pl.ds(0, group - local)], recv_sem.at[k])
        else:
            size = group if turn is None else part
            wait_for(held.at[pl.ds(0, size)], recv_sem.at[rows if turn else k])
        at = piece(source, turn)
        for q in range(last + 1):
            x = jnp.swapaxes(held[at, q * GROUP : (q + 1) * GROUP, :], 0, 1)
            if q == 0:
                edge[0, :, at] = x[:halo]
            if q == last:
                edge[1, :, at] = x[GROUP - halo :]
        for side in range(2):
            @pl.when(relayed(side, row, source))
            def _(side=side):
                relay_copy(side, k, turn).start()
        for q in range(last + 1):
            x = jnp.swapaxes(held[at, q * GROUP : (q + 1) * GROUP, :], 0, 1)
            here = slice(halo + q * GROUP, halo + (q + 1) * GROUP)
            add(here, product(x, at), finish)

    def halo_part(k, finish, turn=None):
        for side in range(2):
            beyond = row + (1 if side else -1)
            source = lax.rem(beyond - k + rows, rows)
            at = piece(source, turn)
            here = slice(halo + tile_rows, 2 * halo + tile_rows) if side else slice(0, halo)

            @pl.when(there(1 if side else -1, rows, row))
            def _(side=side, beyond=beyond, source=source, at=at, here=here):
                direct = jnp.logical_not(relayed(1 - side, beyond, source))

                @pl.when(direct & (not turn))
                def _():
                    slot = source - half * mid

                    @pl.when(source == row)
                    def _():
                        strip_self.wait()
                        wait_for(strip.at[pl.ds(0, group - local)], strip_recv.at[slot])

                    @pl.when(source != row)
                    def _():
                        wait_for(strip.at[pl.ds(0, group)], strip_recv.at[slot])

                    x = jnp.swapaxes(strip[frames_of(slot)], 0, 1)
                    rim[side, :, frames_of(source)] = x[:halo] if side else x[GROUP - halo :]

                @pl.when(jnp.logical_not(direct))
                def _():
                    wait_for(rim.at[side, :, at], relay_recv.at[side, rows if turn else k])

                add(here, product(rim[side, :, at], at), finish)

    visits = order
    for k in visits[:-1]:
        main_part(k, False)
    for k in visits[:-2]:
        halo_part(k, False)
    if final:
        main_part(final, False, 0)
        main_part(final, True, 1)
        halo_part(visits[-2], False)
        halo_part(final, False, 0)
        halo_part(final, True, 1)
    else:
        main_part(final, True)
        halo_part(visits[-2], False)
        halo_part(final, True)

    def side_copy(i):
        return pltpu.make_async_remote_copy(
            src_ref=side_out.at[i], dst_ref=side_in.at[1 - i],
            send_sem=side_send.at[i], recv_sem=side_recv.at[1 - i],
            device_id=(row, col + (1 if i else -1)), device_id_type=MESH,
        )

    for i in range(2):
        for j in range(halo):
            at = PAD + j + (tile_cols - halo if i else 0)
            for c in range(chunks):
                side_out[i, j, c] = flux[c, :, at, :]
    for i in range(2):
        @pl.when(there(1 if i else -1, cols, col))
        def _(i=i):
            side_copy(i).start()

    wait_for(held.at[pl.ds(0, total - local)], send_sem)

    @pl.when(beside)
    def _():
        wait_for(strip.at[pl.ds(0, group - local)], strip_send)

    @pl.when(jnp.logical_not(beside))
    def _():
        wait_for(strip.at[pl.ds(0, group)], strip_send)

    for k in range(rows):
        for side in range(2):
            @pl.when(relayed(side, row, lax.rem(row - k + rows, rows)))
            def _(side=side, k=k):
                for turn in (0, 1) if k and k == final else (None,):
                    relay_copy(side, k, turn).wait_send()
    for i in range(2):
        @pl.when(there(1 if i else -1, cols, col))
        def _(i=i):
            side_copy(i).wait_send()
            wait_for(side_in.at[i], side_recv.at[i])
            for j in range(halo):
                at = PAD + tile_cols + j if i else PAD - halo + j
                for c in range(chunks):
                    flux[c, :, at, :] = side_in[i, j, c]


def relax_kernel(flux, wide, out, first, second, third, sem):
    chunks, count, width = flux.shape[0], flux.shape[1], flux.shape[2]

    def out_copy(c):
        return pltpu.make_async_copy(
            third.at[c], out.at[:, :, c * LANES : (c + 1) * LANES], sem.at[c]
        )

    for c in range(chunks):
        source = flux.at[c]
        for step, target in enumerate((first, second, None)):
            if target is None:
                bounds = [PAD, PAD + (width - 2 * PAD) // 2, width - PAD]
            else:
                bounds = [1 + step, width // 2, width - 1 - step]
            for a, b in zip(bounds[:-1], bounds[1:]):
                above, center = source[step, a:b, :], source[step + 1, a:b, :]
                for h in range(step + 1, count - step - 1):
                    below = source[h + 1, a:b, :]
                    laplace = (
                        below + above
                        + source[h, a + 1 : b + 1, :] + source[h, a - 1 : b - 1, :] - 4.0 * center
                    )
                    value = center + wide[h, a:b, :] * laplace
                    if target is None:
                        third[c, h - PASSES, a - PAD : b - PAD] = value
                    else:
                        target[h, a:b, :] = value
                    above, center = center, below
            source = target
        out_copy(c).start()
    for c in range(chunks):
        out_copy(c).wait()


def per_device(frames, class_index, surface_mask, effusivity, conductivity):
    rows = lax.axis_size("row")
    cols = lax.axis_size("col")
    local, height, width = frames.shape
    tile_rows, tile_cols = height // rows, width // cols
    total = local * rows * cols
    if rows % 2 or cols % 2 or local % 8 or tile_rows % GROUP or tile_cols != LANES or total % LANES or (local * cols) % LANES or local * cols % 32:
        return plain_device(frames, class_index, surface_mask, effusivity, conductivity)
    chunks = total // LANES
    high_rows, wide_cols = tile_rows + 2 * PASSES, tile_cols + 2 * PAD
    vmem = pl.BlockSpec(memory_space=pltpu.VMEM)
    smem = pl.BlockSpec(memory_space=pltpu.SMEM)
    dma = pltpu.SemaphoreType.DMA
    sides = len(SIDES)
    arguments = (frames, class_index, surface_mask, effusivity, conductivity)
    flux, wide = pl.pallas_call(
        functools.partial(gather_kernel, rows, cols, tile_rows, tile_cols, local),
        out_shape=(
            jax.ShapeDtypeStruct((chunks, high_rows, wide_cols, LANES), jnp.float32),
            jax.ShapeDtypeStruct((high_rows, wide_cols, LANES), jnp.float32),
        ),
        in_specs=[pl.BlockSpec(memory_space=pltpu.HBM), vmem, vmem, smem, smem],
        out_specs=(vmem, vmem),
        scratch_shapes=[
            pltpu.VMEM((total, tile_rows, tile_cols), jnp.float32),
            pltpu.VMEM((2, tile_rows, tile_cols), jnp.float32),
            pltpu.VMEM((sides, 2, tile_rows, tile_cols), jnp.float32),
            pltpu.VMEM((high_rows, tile_cols, LANES), jnp.float32),
            pltpu.VMEM((2, total, total), jnp.bfloat16),
            pltpu.VMEM((2, PASSES, total, tile_cols), jnp.float32),
            pltpu.VMEM((2, PASSES, total, tile_cols), jnp.float32),
            pltpu.VMEM((total // 2, GROUP, tile_cols), jnp.float32),
            pltpu.VMEM((2, PASSES, chunks, high_rows, LANES), jnp.float32),
            pltpu.VMEM((2, PASSES, chunks, high_rows, LANES), jnp.float32),
            dma, dma((rows + 1,)), dma, dma((sides,)), dma((sides,)),
            dma, dma((rows // 2,)), dma, dma((2, rows + 1)), dma((2, rows + 1)), dma((2,)), dma((2,)),
        ],
        compiler_params=pltpu.CompilerParams(
            collective_id=0, has_side_effects=True, vmem_limit_bytes=VMEM_GATHER
        ),
        name="gather",
    )(*(pltpu.with_memory_space_constraint(x, pltpu.HBM) for x in arguments))
    return pl.pallas_call(
        relax_kernel,
        out_shape=jax.ShapeDtypeStruct((tile_rows, tile_cols, total), jnp.float32),
        in_specs=[vmem, vmem],
        out_specs=pl.BlockSpec(memory_space=pltpu.HBM),
        scratch_shapes=[pltpu.VMEM((high_rows, wide_cols, LANES), jnp.float32)] * 2
        + [pltpu.VMEM((chunks, tile_rows, tile_cols, LANES), jnp.float32), dma((chunks,))],
        compiler_params=pltpu.CompilerParams(vmem_limit_bytes=24 * 2**20),
        name="relax",
    )(flux, wide)


def solution(mesh):
    in_specs = (P(("row", "col"), None, None), P("row", "col"), P("row", "col"), P(), P())
    out_specs = P("row", "col", None)
    return jax.shard_map(
        per_device, mesh=mesh, in_specs=in_specs, out_specs=out_specs, check_vma=False
    )
```
